32 devices in a mesh: sec: 8 (over z, x), tile: 4 (over y, core).
Axes of the slice: x: 2, y: 2, z: 4, core: 2. Of those that a mesh axis runs over, the one named last changes fastest.
Arguments:
- displacement: float32 [2, 8, 1024, 2048], P(None, 'sec', 'tile'), may hold values from -6 to 6
- spring: float32 [8, 1024, 2048], P('sec', 'tile'), may hold values from 0.5 to 2
- stiff_table: float32 [8], replicated, may hold values from 0.25 to 2
- match_blocks: int32 [2, 8, 1024], P(None, 'sec', 'tile'), may hold values from 0 to 4095
- match_class: int32 [8, 1024], P('sec', 'tile'), may hold values from 0 to 7
Outputs:
- relaxed: float32 [2, 8, 1024, 2048], P(None, 'sec', 'tile')
The draws below stay inside these ranges and needn't reach their ends.
All inputs are finite; a program needn't handle non-finite values.
Results may differ from the reference program's by a relative error of at most 0.000053.
Values sent between devices are 32-bit elements; how exact they have to be, the bound alone decides.
No kernel may reach another device: no remote copies, remote signals or barrier semaphores. Data moves between devices by JAX's collectives and lax.ppermute only.
A program may use at most 128 MiB of HBM per device.

```python
import math
import jax
import jax.numpy as jnp

R_DEV = 256
COLS = 2048
MAXM = 256
NCLASS = 8
ITERS = 3
NSEC = 8
ROWS = 1024
NBLK = 4096
N_TILE = 4


def plant(array, key, low, top_value):
    place = [jax.random.randint(jax.random.fold_in(key, axis), (), 0, length) for axis, length in enumerate(array.shape)]
    widest = array.shape.index(max(array.shape))
    beside = place[:widest] + [(place[widest] + 1) % array.shape[widest]] + place[widest + 1:]
    return array.at[tuple(place)].set(low).at[tuple(beside)].set(top_value)


def steps_of(rng, dims, split, least, high):
    def one(dim, blocks):
        draws = jax.random.uniform(jax.random.fold_in(jax.random.fold_in(rng, 6), dim), (blocks,), jnp.float32, least / len(split), high / len(split))
        return jnp.repeat(jnp.exp(draws), dims[dim] // blocks).reshape((-1,) + (1,) * (len(dims) - dim - 1))

    gain = one(*split[0])
    for cut in split[1:]:
        gain = gain * one(*cut)
    return gain


def normal_values(stream_key, extent, spread, limit, cuts=(), kind=jnp.bfloat16):
    gain = steps_of(stream_key, extent, cuts, -0.22, 0.18) if cuts else 1.0
    values = jax.random.normal(stream_key, extent, jnp.float32) * spread * gain
    return jnp.minimum(jnp.maximum(values, -limit), limit).astype(kind)


def setup_inputs(seed: int = 0) -> dict:
    streams_of = jax.random.split(jax.random.key(seed), 6)
    return {
        "displacement": normal_values(streams_of[0], (2, NSEC, ROWS, COLS), 1.0, 6.0, ((1, 8), (2, 4)), jnp.float32),
        "spring": jnp.clip(jnp.exp(math.log(2.0) - 1.3862944 * jax.random.uniform(streams_of[1], (NSEC, ROWS, COLS), jnp.float32) ** steps_of(streams_of[1], (NSEC, ROWS, COLS), ((0, 8), (1, 4)), -0.2, 0.2)), 0.5, 2.0),
        "stiff_table": jnp.clip(jnp.exp(jax.random.uniform(streams_of[2], (NCLASS,), jnp.float32, math.log(0.25), math.log(2.0))), 0.25, 2.0),
        "match_blocks": plant(jax.random.randint(streams_of[3], (2, NSEC, N_TILE * MAXM), 0, NBLK), jax.random.fold_in(streams_of[3], 1), 0, NBLK - 1).astype(jnp.int32),
        "match_class": plant(jax.random.randint(streams_of[4], (NSEC, N_TILE * MAXM), 0, NCLASS), jax.random.fold_in(streams_of[4], 1), 0, NCLASS - 1).astype(jnp.int32),
    }


def reference(displacement, spring, stiff_table, match_blocks, match_class):
    block_count = R_DEV * COLS // 128
    sections = jnp.arange(NSEC, dtype=jnp.int32)[:, None, None]
    bands = jnp.arange(N_TILE, dtype=jnp.int32)[None, :, None]
    source = match_blocks[0].reshape(NSEC, N_TILE, MAXM)
    target = match_blocks[1].reshape(NSEC, N_TILE, MAXM)
    classes_in = match_class.reshape(NSEC, N_TILE, MAXM)
    alive = (sections < NSEC - 1).astype(jnp.float32)
    coupling = (stiff_table[classes_in] * alive).reshape(-1)
    following = jnp.minimum(sections + 1, NSEC - 1)
    global_source = ((sections * N_TILE + bands) * block_count + source).reshape(-1).astype(jnp.int32)
    global_target = ((following * N_TILE + bands) * block_count + target).reshape(-1).astype(jnp.int32)
    total_blocks = NSEC * N_TILE * block_count
    diag_blocks = jnp.zeros((total_blocks,), jnp.float32).at[global_source].add(coupling).at[global_target].add(coupling)
    diagonal = 4.0 * spring + jnp.repeat(diag_blocks.reshape(NSEC, ROWS, COLS // 128), 128, axis=2)
    field = displacement
    for sweep in range(ITERS):
        blocked = field.reshape(2, total_blocks, 128)
        at_source = blocked[:, global_source]
        at_target = blocked[:, global_target]
        term_match = coupling[None, :, None] * (at_target - at_source)
        matched = jnp.zeros_like(blocked).at[:, global_source].add(term_match).at[:, global_target].add(-term_match)
        padded = jnp.pad(field, ((0, 0), (0, 0), (1, 1), (1, 1)))
        laplace = padded[:, :, 2:, 1:-1] + padded[:, :, :-2, 1:-1] + padded[:, :, 1:-1, 2:] + padded[:, :, 1:-1, :-2] - 4.0 * field
        force = spring[None] * laplace + matched.reshape(field.shape)
        field = field + 0.8 * force / diagonal[None]
    return field
```

```python
import functools
import jax
import jax.numpy as jnp
from jax import lax
from jax.experimental import pallas as pl
from jax.experimental.pallas import tpu as pltpu
from jax.sharding import PartitionSpec as P

ITERS = 3
LANES = 128
SUB = 8
GUARD = 8

VM = pl.BlockSpec(memory_space=pltpu.VMEM)
SM = pl.BlockSpec(memory_space=pltpu.SMEM)
ANY = pl.BlockSpec(memory_space=pl.ANY)


def f32(*shape):
    return jax.ShapeDtypeStruct(shape, jnp.float32)


def tile_row(block, chunks):
    row = block // chunks
    return (row // SUB) * (SUB * chunks) + (block % chunks) * SUB + row % SUB


def pieces(x):
    high = x.astype(jnp.bfloat16)
    low = (x - high.astype(jnp.float32)).astype(jnp.bfloat16)
    return high, low


def summed(same, x):
    high, low = pieces(x)
    return jnp.dot(same, high, preferred_element_type=jnp.float32) + jnp.dot(
        same, low, preferred_element_type=jnp.float32
    )


def send_edges(flags, entry, halo_a, halo_b, count, chunks):
    odd_tile = flags[1]
    low = pl.multiple_of(count + (1 - odd_tile) * chunks, SUB)
    high = pl.multiple_of(count + odd_tile * chunks, SUB)
    halo_a[...] = entry[:, pl.ds(low, chunks), :]
    halo_b[...] = entry[:, pl.ds(high, chunks), :]


def first_kernel(matches, chunks, flags, own, own_class, prev, table, field, entry, rows, stiff, send_x, send_z, halo_a, halo_b, held, sem):
    blocks = held.shape[1]
    count = 2 * matches
    copy = pltpu.make_async_copy(field, held, sem)
    copy.start()
    odd = flags[0]
    own_at = odd * matches
    prev_at = matches - own_at
    alive = flags[2].astype(jnp.float32)
    alive_before = flags[3].astype(jnp.float32)
    copy.wait()

    def place(slot, block, level, on):
        row = tile_row(block, chunks)
        rows[slot] = row
        stiff[pl.ds(slot, 1), :] = jnp.full((1, LANES), table[level] * on, jnp.float32)
        for part in range(2):
            entry[part, pl.ds(slot, 1), :] = held[part, pl.ds(row, 1), :]

    def some(step, carry):
        for inner in range(4):
            j = step * 4 + inner
            place(own_at + j, own[0, 0, j], own_class[0, j], alive)
            place(prev_at + j, prev[0, j], prev[1, j], alive_before)
        return carry

    lax.fori_loop(0, matches // 4, some, 0)
    for part in range(2):
        for chunk in range(chunks):
            entry[part, pl.ds(count + chunk, 1), :] = held[part, pl.ds(chunk * SUB, 1), :]
            entry[part, pl.ds(count + chunks + chunk, 1), :] = held[
                part, pl.ds(blocks - SUB * chunks + chunk * SUB + SUB - 1, 1), :
            ]
        send_x[part] = entry[part, :matches, :] * stiff[:matches, :]
        send_z[part] = entry[part, matches:count, :] * stiff[matches:, :]
    send_edges(flags, entry, halo_a, halo_b, count, chunks)


def setup_kernel(matches, chunks, flags, rows, own, own_class, prev, table, stiff, spring, same, weight, factor, held, picked, column, sem):
    blocks = held.shape[0]
    count = 2 * matches
    total = count + 2 * chunks
    copy = pltpu.make_async_copy(spring, held, sem)
    copy.start()
    odd = flags[0]

    def levels(classes):
        out = jnp.zeros(classes.shape, jnp.float32)
        for level in range(table.shape[0]):
            out = jnp.where(classes == level, table[level], out)
        return out

    coupling_own = levels(own_class[...]) * flags[2].astype(jnp.float32)
    coupling_prev = levels(prev[1:2, :]) * flags[3].astype(jnp.float32)
    rows_own = tile_row(own[0], chunks)
    rows_prev = tile_row(prev[0:1, :], chunks)
    first = odd == 0
    rows_line = jnp.concatenate(
        [jnp.where(first, rows_own, rows_prev), jnp.where(first, rows_prev, rows_own)], axis=1
    )
    stiff_line = jnp.concatenate(
        [jnp.where(first, coupling_own, coupling_prev), jnp.where(first, coupling_prev, coupling_own)],
        axis=1,
    )
    copy.wait()

    def take(slot, row):
        picked[pl.ds(slot, 1), :] = held[pl.ds(row, 1), :]
        column[pl.ds(slot, 1), :] = jnp.full((1, LANES), row, jnp.int32)

    def some(step, carry):
        for inner in range(8):
            slot = step * 8 + inner
            take(slot, rows[slot])
        return carry

    lax.fori_loop(0, count // 8, some, 0)
    for chunk in range(chunks):
        take(count + chunk, chunk * SUB)
        take(count + chunks + chunk, blocks - SUB * chunks + chunk * SUB + SUB - 1)

    def band(step, carry):
        at = pl.ds(pl.multiple_of(step * 32, 32), 32)
        col = column[at, :]
        total_stiff = jnp.zeros((32, 1), jnp.float32)
        for piece in range(count // LANES):
            cut = slice(piece * LANES, (piece + 1) * LANES)
            equal = col == rows_line[:, cut]
            same[at, cut] = equal.astype(jnp.float32).astype(jnp.bfloat16)
            total_stiff += jnp.sum(jnp.where(equal, stiff_line[:, cut], 0.0), axis=1, keepdims=True)
        spring_here = picked[at, :]
        inverse = 1.0 / (4.0 * spring_here + total_stiff)
        weight[at, :] = 4.0 * spring_here * inverse
        factor[at, :] = 0.8 * inverse
        return carry

    lax.fori_loop(0, total // 32, band, 0)


def bulk_kernel(matches, chunks, scatter, flags, rows, field, entry, got_a, got_b, same, stiff, weight, factor, nearby, base, padded, sem):
    blocks = field.shape[1]
    count = 2 * matches
    span = SUB * chunks
    pad = GUARD + span
    copies = [
        pltpu.make_async_copy(field.at[part], padded.at[part, pl.ds(pad, blocks), :], sem.at[part])
        for part in range(2)
    ]
    for copy in copies:
        copy.start()
    odd_tile = flags[1] == 1
    for part in range(2):
        a, b = got_a[part], got_b[part]
        above = jnp.where(odd_tile, a, b)
        below = jnp.where(odd_tile, b, a)
        for chunk in range(chunks):
            padded[part, pl.ds(GUARD + chunk * SUB + SUB - 1, 1), :] = above[chunk : chunk + 1, :]
            padded[part, pl.ds(pad + blocks + chunk * SUB, 1), :] = below[chunk : chunk + 1, :]
    for copy in copies:
        copy.wait()
    if scatter:

        def put(step, carry):
            for inner in range(8):
                slot = step * 8 + inner
                row = rows[slot] + pad
                for part in range(2):
                    padded[part, pl.ds(row, 1), :] = entry[part, pl.ds(slot, 1), :]
            return carry

        lax.fori_loop(0, count // 8, put, 0)

    lane = lax.broadcasted_iota(jnp.int32, (SUB, LANES), 1)
    sub = lax.broadcasted_iota(jnp.int32, (SUB, LANES), 0)
    is_first, is_last = lane == 0, lane == LANES - 1
    is_top, is_bottom = sub == 0, sub == SUB - 1

    def strip(step, carry):
        start = pl.multiple_of(step * span, SUB)
        for part in range(2):

            def at(offset):
                return padded[part, pl.ds(start + (pad + offset), SUB), :]

            before = jnp.zeros((SUB, LANES), jnp.float32)
            here = at(0)
            for chunk in range(chunks):
                offset = chunk * SUB
                after = at(offset + SUB) if chunk < chunks - 1 else jnp.zeros((SUB, LANES), jnp.float32)
                up = jnp.where(is_top, at(offset - span + SUB - 1), at(offset - 1))
                down = jnp.where(is_bottom, at(offset + span - SUB + 1), at(offset + 1))
                left = pltpu.roll(jnp.where(is_last, before, here), 1, 1)
                right = pltpu.roll(jnp.where(is_first, after, here), LANES - 1, 1)
                nearby[part, pl.ds(start + offset, SUB), :] = 0.2 * (((up + down) + (left + right)) + here)
                before, here = here, after
        return carry

    lax.fori_loop(0, blocks // span, strip, 0)

    def take(slot, row):
        for part in range(2):
            base[part, pl.ds(slot, 1), :] = nearby[part, pl.ds(row, 1), :]

    def some(step, carry):
        for inner in range(8):
            slot = step * 8 + inner
            take(slot, rows[slot])
        return carry

    lax.fori_loop(0, count // 8, some, 0)
    for chunk in range(chunks):
        take(count + chunk, chunk * SUB)
        take(count + chunks + chunk, blocks - span + chunk * SUB + SUB - 1)
    own = jnp.concatenate([entry[part, :count, :] * stiff[...] for part in range(2)], axis=1)
    total = summed(same[...], own)
    for part in range(2):
        value = entry[part]
        base[part] = (
            value
            + weight[...] * (base[part] - value)
            - factor[...] * total[:, part * LANES : (part + 1) * LANES]
        )


def new_entries(got_x, got_z, base, same, factor):
    got = jnp.concatenate(
        [jnp.concatenate([got_x[part], got_z[part]], axis=0) for part in range(2)], axis=1
    )
    total = summed(same[...], got)
    return [base[part] + factor[...] * total[:, part * LANES : (part + 1) * LANES] for part in range(2)]


def step_kernel(matches, chunks, flags, got_x, got_z, base, same, factor, stiff, entry, send_x, send_z, halo_a, halo_b):
    count = 2 * matches
    for part, value in enumerate(new_entries(got_x, got_z, base, same, factor)):
        entry[part] = value
        send_x[part] = value[:matches] * stiff[:matches, :]
        send_z[part] = value[matches:count] * stiff[matches:, :]
    send_edges(flags, entry, halo_a, halo_b, count, chunks)


def last_kernel(matches, chunks, rows, nearby, got_x, got_z, base, same, factor, out, held, entry, sem):
    count = 2 * matches
    loads = [pltpu.make_async_copy(nearby.at[part], held.at[part], sem.at[part]) for part in range(2)]
    for copy in loads:
        copy.start()
    for part, value in enumerate(new_entries(got_x, got_z, base, same, factor)):
        entry[part] = value
    stores = []
    for part in range(2):
        loads[part].wait()

        def put(step, carry):
            for inner in range(8):
                slot = step * 8 + inner
                held[part, pl.ds(rows[slot], 1), :] = entry[part, pl.ds(slot, 1), :]
            return carry

        lax.fori_loop(0, count // 8, put, 0)
        stores.append(pltpu.make_async_copy(held.at[part], out.at[part], sem.at[2 + part]))
        stores[-1].start()
    for copy in stores:
        copy.wait()


def exchange(array, axis, pairs):
    return lax.ppermute(array, axis, pairs)


def pairs_from(first, size):
    out = []
    for i in range(first, size - 1, 2):
        out += [(i, i + 1), (i + 1, i)]
    return out


def on_device(displacement, spring, stiff_table, match_blocks, match_class):
    fields, single, height, breadth = displacement.shape
    chunks = breadth // LANES
    blocks = height * chunks
    matches = match_blocks.shape[2]
    count = 2 * matches
    total = count + 2 * chunks
    section, sections = lax.axis_index("sec"), lax.axis_size("sec")
    tile, tiles = lax.axis_index("tile"), lax.axis_size("tile")
    near, far = pairs_from(0, sections), pairs_from(1, sections)
    near_tile, far_tile = pairs_from(0, tiles), pairs_from(1, tiles)

    def tiled(x):
        lead = x.shape[:-2]
        x = x.reshape(lead + (height // SUB, SUB, chunks, LANES))
        return jnp.swapaxes(x, -3, -2).reshape(lead + (blocks, LANES))

    def untiled(x):
        lead = x.shape[:-2]
        x = x.reshape(lead + (height // SUB, chunks, SUB, LANES))
        return jnp.swapaxes(x, -3, -2).reshape(lead + (height, breadth))

    flags = jnp.stack(
        [section % 2, tile % 2, (section < sections - 1).astype(jnp.int32), (section > 0).astype(jnp.int32)]
    )
    prev = exchange(
        jnp.concatenate([match_blocks[1], match_class], axis=0),
        "sec",
        [(i, i + 1) for i in range(sections - 1)],
    )
    field = tiled(displacement[:, 0])
    params = pltpu.CompilerParams(vmem_limit_bytes=24 << 20)
    halo = f32(fields, chunks, LANES)
    send = f32(fields, matches, LANES)
    entries = f32(fields, total, LANES)
    big = f32(fields, blocks, LANES)

    entry, rows, stiff, send_x, send_z, halo_a, halo_b = pl.pallas_call(
        functools.partial(first_kernel, matches, chunks),
        out_shape=(entries, jax.ShapeDtypeStruct((count,), jnp.int32), f32(count, LANES), send, send, halo, halo),
        in_specs=[SM, SM, SM, SM, SM, ANY],
        out_specs=(VM, SM, VM, VM, VM, VM, VM),
        scratch_shapes=[pltpu.VMEM((fields, blocks, LANES), jnp.float32), pltpu.SemaphoreType.DMA],
        compiler_params=params,
        name="first",
    )(flags, match_blocks[:1], match_class, prev, stiff_table, field)

    for sweep in range(ITERS):
        got_x = exchange(send_x, "sec", near)
        got_z = exchange(send_z, "sec", far)
        got_a = exchange(halo_a, "tile", near_tile)
        got_b = exchange(halo_b, "tile", far_tile)
        if sweep == 0:
            same, weight, factor = pl.pallas_call(
                functools.partial(setup_kernel, matches, chunks),
                out_shape=(
                    jax.ShapeDtypeStruct((total, count), jnp.bfloat16),
                    f32(total, LANES),
                    f32(total, LANES),
                ),
                in_specs=[SM, SM, VM, VM, VM, SM, VM, ANY],
                out_specs=(VM, VM, VM),
                scratch_shapes=[
                    pltpu.VMEM((blocks, LANES), jnp.float32),
                    pltpu.VMEM((total, LANES), jnp.float32),
                    pltpu.VMEM((total, LANES), jnp.int32),
                    pltpu.SemaphoreType.DMA,
                ],
                compiler_params=params,
                name="setup",
            )(flags, rows, match_blocks[:1, 0], match_class, prev, stiff_table, stiff, tiled(spring[0]))
        field, base = pl.pallas_call(
            functools.partial(bulk_kernel, matches, chunks, sweep > 0),
            out_shape=(big, entries),
            in_specs=[SM, SM, ANY] + [VM] * 7,
            out_specs=(VM, VM),
            scratch_shapes=[
                pltpu.VMEM((fields, blocks + 2 * (GUARD + SUB * chunks), LANES), jnp.float32),
                pltpu.SemaphoreType.DMA((2,)),
            ],
            compiler_params=params,
            name="bulk",
        )(flags, rows, field, entry, got_a, got_b, same, stiff, weight, factor)
        if sweep < ITERS - 1:
            entry, send_x, send_z, halo_a, halo_b = pl.pallas_call(
                functools.partial(step_kernel, matches, chunks),
                out_shape=(entries, send, send, halo, halo),
                in_specs=[SM] + [VM] * 6,
                out_specs=(VM,) * 5,
                compiler_params=params,
                name="step",
            )(flags, got_x, got_z, base, same, factor, stiff)
        else:
            field = pl.pallas_call(
                functools.partial(last_kernel, matches, chunks),
                out_shape=big,
                in_specs=[SM, ANY] + [VM] * 5,
                out_specs=ANY,
                scratch_shapes=[
                    pltpu.VMEM((fields, blocks, LANES), jnp.float32),
                    pltpu.VMEM((fields, total, LANES), jnp.float32),
                    pltpu.SemaphoreType.DMA((4,)),
                ],
                compiler_params=params,
                name="last",
            )(rows, field, got_x, got_z, base, same, factor)
    return untiled(field)[:, None]


def solution(mesh):
    placed = (
        P(None, "sec", "tile", None),
        P("sec", "tile", None),
        P(),
        P(None, "sec", "tile"),
        P("sec", "tile"),
    )
    return jax.shard_map(
        on_device,
        mesh=mesh,
        in_specs=placed,
        out_specs=P(None, "sec", "tile", None),
        check_vma=False,
    )
```

```python
import functools
import jax
import jax.numpy as jnp
from jax import lax
from jax.experimental import pallas as pl
from jax.experimental.pallas import tpu as pltpu
from jax.sharding import PartitionSpec as P

ITERS = 3
LANES = 128
SUB = 8

VM = pl.BlockSpec(memory_space=pltpu.VMEM)
SM = pl.BlockSpec(memory_space=pltpu.SMEM)
HBM = pl.BlockSpec(memory_space=pltpu.MemorySpace.HBM)


def f32(*shape):
    return jax.ShapeDtypeStruct(shape, jnp.float32)


def tile_row(block, chunks):
    row = block // chunks
    return (row // SUB) * (SUB * chunks) + (block % chunks) * SUB + row % SUB


def pieces(x):
    high = x.astype(jnp.bfloat16)
    low = (x - high.astype(jnp.float32)).astype(jnp.bfloat16)
    return high, low


def summed(same, x):
    high, low = pieces(x)
    return jnp.dot(same, high, preferred_element_type=jnp.float32) + jnp.dot(
        same, low, preferred_element_type=jnp.float32
    )


def parity(axis):
    return lax.axis_index(axis) % 2


def send_edges(entry, halo_a, halo_b, count, chunks):
    odd_tile = parity("tile")
    low = pl.multiple_of(count + (1 - odd_tile) * chunks, SUB)
    high = pl.multiple_of(count + odd_tile * chunks, SUB)
    halo_a[...] = entry[:, pl.ds(low, chunks), :]
    halo_b[...] = entry[:, pl.ds(high, chunks), :]


def levels(classes, table, alive):
    out = jnp.zeros(classes.shape, jnp.float32)
    for level in range(table.shape[0]):
        out = jnp.where(classes == level, table[level], out)
    return out * alive.astype(jnp.float32)


def columns(line):
    return jnp.concatenate(
        [
            jnp.broadcast_to(line[:, at : at + LANES], (LANES, LANES)).T
            for at in range(0, line.shape[1], LANES)
        ],
        axis=0,
    )


def each_slot(count, rows, body):
    def some(step, carry):
        for inner in range(8):
            slot = step * 8 + inner
            body(slot, rows(slot))
        return carry

    lax.fori_loop(0, count // 8, some, 0)


def own_kernel(own, table, classes, displacement, field, entry, stiff, line, level, classes_in, sem):
    copies = [
        pltpu.make_async_copy(displacement, field, sem.at[0]),
        pltpu.make_async_copy(table, level, sem.at[1]),
        pltpu.make_async_copy(classes, classes_in, sem.at[2]),
    ]
    for copy in copies:
        copy.start()
    copies[1].wait()
    copies[2].wait()
    alive = lax.axis_index("sec") < lax.axis_size("sec") - 1
    line[...] = levels(classes_in[...], level, alive)
    stiff[...] = columns(line[...])
    copies[0].wait()

    def take(slot, row):
        for part in range(2):
            entry[part, pl.ds(slot, 1), :] = field[part, pl.ds(row, 1), :]

    each_slot(own.shape[1], lambda j: own[0, j], take)


def first_kernel(chunks, prev, prev_line, own_line, table, field, own_entry, own_stiff, own_stiff_line, entry, stiff, rows, stiff_line, send_x, send_z, halo_a, halo_b):
    blocks = field.shape[1]
    matches = own_entry.shape[1]
    count = 2 * matches
    odd = parity("sec")
    own_at = pl.multiple_of(odd * matches, LANES)
    prev_at = pl.multiple_of((1 - odd) * matches, LANES)

    def take(slot, row):
        for part in range(2):
            entry[part, pl.ds(prev_at + slot, 1), :] = field[part, pl.ds(row, 1), :]

    each_slot(matches, lambda j: prev[0, j], take)
    line = levels(prev_line[1:2, :], table, lax.axis_index("sec") > 0)
    stiff[pl.ds(prev_at, matches), :] = columns(line)
    stiff[pl.ds(own_at, matches), :] = own_stiff[...]
    entry[:, pl.ds(own_at, matches), :] = own_entry[...]
    even = odd == 0
    for out, first, second in ((rows, own_line[...], prev_line[0:1, :]), (stiff_line, own_stiff_line[...], line)):
        out[:, :matches] = jnp.where(even, first, second)
        out[:, matches:] = jnp.where(even, second, first)
    for part in range(2):
        for chunk in range(chunks):
            entry[part, pl.ds(count + chunk, 1), :] = field[part, pl.ds(chunk * SUB, 1), :]
            entry[part, pl.ds(count + chunks + chunk, 1), :] = field[
                part, pl.ds(blocks - SUB * chunks + chunk * SUB + SUB - 1, 1), :
            ]
        send_x[part] = entry[part, :matches, :] * stiff[:matches, :]
        send_z[part] = entry[part, matches:count, :] * stiff[matches:, :]
    send_edges(entry, halo_a, halo_b, count, chunks)


def setup_kernel(chunks, rows, rows_line, stiff_line, spring, same, weight, factor, held, picked, column, sem):
    blocks = held.shape[0]
    count = rows_line.shape[1]
    total = count + 2 * chunks
    copy = pltpu.make_async_copy(spring, held, sem)
    copy.start()
    line = rows_line[...].astype(jnp.float32)
    column[:count, :] = columns(line)
    edge = lax.broadcasted_iota(jnp.int32, (chunks, LANES), 0) * SUB
    column[count : count + chunks, :] = edge.astype(jnp.float32)
    column[count + chunks :, :] = (edge + (blocks - SUB * chunks + SUB - 1)).astype(jnp.float32)

    def band(step, carry):
        at = pl.ds(pl.multiple_of(step * 32, 32), 32)
        col = column[at, :]
        total_stiff = jnp.zeros((32, LANES), jnp.float32)
        for piece in range(count // LANES):
            cut = slice(piece * LANES, (piece + 1) * LANES)
            equal = col == rows_line[:, cut].astype(jnp.float32)
            same[at, cut] = equal.astype(jnp.float32).astype(jnp.bfloat16)
            total_stiff += jnp.where(equal, stiff_line[:, cut], 0.0)
        factor[at, :] = jnp.broadcast_to(jnp.sum(total_stiff, axis=1, keepdims=True), (32, LANES))
        return carry

    lax.fori_loop(0, total // 32, band, 0)
    copy.wait()

    def take(slot, row):
        picked[pl.ds(slot, 1), :] = held[pl.ds(row, 1), :]

    each_slot(count, lambda j: rows[0, j], take)
    for chunk in range(chunks):
        take(count + chunk, chunk * SUB)
        take(count + chunks + chunk, blocks - SUB * chunks + chunk * SUB + SUB - 1)
    spring_here = picked[...]
    inverse = 1.0 / (4.0 * spring_here + factor[...])
    weight[...] = 4.0 * spring_here * inverse
    factor[...] = 0.8 * inverse


def stencil(field, nearby, start, chunks, above=None, below=None):
    span = SUB * chunks
    lane = lax.broadcasted_iota(jnp.int32, (SUB, LANES), 1)
    sub = lax.broadcasted_iota(jnp.int32, (SUB, LANES), 0)
    for part in range(2):

        def at(offset):
            return field[part, pl.ds(start + offset, SUB), :]

        def edge(halo, chunk):
            return jnp.broadcast_to(halo[part][chunk : chunk + 1, :], (SUB, LANES))

        before = jnp.zeros((SUB, LANES), jnp.float32)
        here = at(0)
        for chunk in range(chunks):
            offset = chunk * SUB
            after = at(offset + SUB) if chunk < chunks - 1 else jnp.zeros((SUB, LANES), jnp.float32)
            if above is None:
                up = jnp.where(sub == 0, at(offset - span + SUB - 1), at(offset - 1))
            else:
                up = jnp.where(sub == 0, edge(above, chunk), pltpu.roll(here, 1, 0))
            if below is None:
                down = jnp.where(sub == SUB - 1, at(offset + span - SUB + 1), at(offset + 1))
            else:
                down = jnp.where(sub == SUB - 1, edge(below, chunk), pltpu.roll(here, SUB - 1, 0))
            left = pltpu.roll(jnp.where(lane == LANES - 1, before, here), 1, 1)
            right = pltpu.roll(jnp.where(lane == 0, after, here), LANES - 1, 1)
            nearby[part, pl.ds(start + offset, SUB), :] = 0.2 * (((up + down) + (left + right)) + here)
            before, here = here, after


def inner_strips(field, nearby, chunks):
    span = SUB * chunks
    strips = field.shape[1] // span

    def pair(step, carry):
        for inner in range(2):
            stencil(field, nearby, pl.multiple_of((1 + step * 2 + inner) * span, SUB), chunks)
        return carry

    lax.fori_loop(0, (strips - 2) // 2, pair, 0)


def inner_kernel(chunks, field, nearby):
    inner_strips(field, nearby, chunks)


def scatter_inner_kernel(chunks, rows, entry, stale, field, nearby):
    def put(slot, row):
        for part in range(2):
            field[part, pl.ds(row, 1), :] = entry[part, pl.ds(slot, 1), :]

    each_slot(rows.shape[1], lambda j: rows[0, j], put)
    inner_strips(field, nearby, chunks)


def edge_kernel(chunks, rows, field, entry, got_a, got_b, same, stiff, weight, factor, partial, nearby, base):
    blocks = field.shape[1]
    span = SUB * chunks
    count = rows.shape[1]
    odd_tile = parity("tile") == 1
    above = [jnp.where(odd_tile, got_a[part], got_b[part]) for part in range(2)]
    below = [jnp.where(odd_tile, got_b[part], got_a[part]) for part in range(2)]
    stencil(field, nearby, 0, chunks, above=above)
    stencil(field, nearby, blocks - span, chunks, below=below)

    def take(slot, row):
        for part in range(2):
            base[part, pl.ds(slot, 1), :] = nearby[part, pl.ds(row, 1), :]

    each_slot(count, lambda j: rows[0, j], take)
    for chunk in range(chunks):
        take(count + chunk, chunk * SUB)
        take(count + chunks + chunk, blocks - span + chunk * SUB + SUB - 1)
    own = jnp.concatenate([entry[part, :count, :] * stiff[...] for part in range(2)], axis=1)
    total = summed(same[...], own)
    for part in range(2):
        value = entry[part]
        base[part] = (
            value
            + weight[...] * (base[part] - value)
            - factor[...] * total[:, part * LANES : (part + 1) * LANES]
        )


def new_entries(got_x, got_z, base, same, factor):
    got = jnp.concatenate(
        [jnp.concatenate([got_x[part], got_z[part]], axis=0) for part in range(2)], axis=1
    )
    total = summed(same[...], got)
    return [base[part] + factor[...] * total[:, part * LANES : (part + 1) * LANES] for part in range(2)]


def step_kernel(chunks, got_x, got_z, base, same, factor, stiff, entry, send_x, send_z, halo_a, halo_b):
    matches = got_x.shape[1]
    count = 2 * matches
    for part, value in enumerate(new_entries(got_x, got_z, base, same, factor)):
        entry[part] = value
        send_x[part] = value[:matches] * stiff[:matches, :]
        send_z[part] = value[matches:count] * stiff[matches:, :]
    send_edges(entry, halo_a, halo_b, count, chunks)


def last_kernel(rows, stale, got_x, got_z, base, same, factor, nearby, out, entry, sem):
    for part, value in enumerate(new_entries(got_x, got_z, base, same, factor)):
        entry[part] = value
    stores = []
    for part in range(2):

        def put(slot, row):
            nearby[part, pl.ds(row, 1), :] = entry[part, pl.ds(slot, 1), :]

        each_slot(rows.shape[1], lambda j: rows[0, j], put)
        stores.append(pltpu.make_async_copy(nearby.at[part], out.at[part], sem.at[part]))
        stores[-1].start()
    for copy in stores:
        copy.wait()


def exchange(array, axis, pairs):
    return lax.ppermute(array, axis, pairs)


def pairs_from(first, size):
    out = []
    for i in range(first, size - 1, 2):
        out += [(i, i + 1), (i + 1, i)]
    return out


def on_device(displacement, spring, stiff_table, match_blocks, match_class):
    fields, single, height, breadth = displacement.shape
    chunks = breadth // LANES
    blocks = height * chunks
    matches = match_blocks.shape[2]
    count = 2 * matches
    total = count + 2 * chunks
    sections, tiles = lax.axis_size("sec"), lax.axis_size("tile")
    near, far = pairs_from(0, sections), pairs_from(1, sections)
    near_tile, far_tile = pairs_from(0, tiles), pairs_from(1, tiles)

    def tiled(x):
        lead = x.shape[:-2]
        x = x.reshape(lead + (height // SUB, SUB, chunks, LANES))
        return jnp.swapaxes(x, -3, -2).reshape(lead + (blocks, LANES))

    def untiled(x):
        lead = x.shape[:-2]
        x = x.reshape(lead + (height // SUB, chunks, SUB, LANES))
        return jnp.swapaxes(x, -3, -2).reshape(lead + (height, breadth))

    def call(name, kernel, ins, outs, **more):
        return pl.pallas_call(
            kernel,
            in_specs=ins,
            out_specs=tuple(spec for spec, _ in outs),
            out_shape=tuple(shape for _, shape in outs),
            compiler_params=pltpu.CompilerParams(vmem_limit_bytes=24 << 20),
            name=name,
            **more,
        )

    halo = (VM, f32(fields, chunks, LANES))
    send = (VM, f32(fields, matches, LANES))
    entries = (VM, f32(fields, total, LANES))
    big = (VM, f32(fields, blocks, LANES))
    wide = (VM, f32(total, LANES))
    rows_shape = (VM, jax.ShapeDtypeStruct((1, count), jnp.int32))

    places = tile_row(match_blocks, chunks)
    own = places[0]
    prev = exchange(
        jnp.concatenate([places[1], match_class], axis=0), "sec", [(i, i + 1) for i in range(sections - 1)]
    )
    field, own_entry, own_stiff, own_stiff_line = call(
        "own",
        own_kernel,
        [SM, HBM, HBM, HBM],
        [big, send, (VM, f32(matches, LANES)), (VM, f32(1, matches))],
        scratch_shapes=[
            pltpu.SMEM(stiff_table.shape, jnp.float32),
            pltpu.VMEM(match_class.shape, jnp.int32),
            pltpu.SemaphoreType.DMA((3,)),
        ],
    )(own, stiff_table, match_class, tiled(displacement[:, 0]))
    entry, stiff, rows, stiff_line, send_x, send_z, halo_a, halo_b = call(
        "first",
        functools.partial(first_kernel, chunks),
        [SM, VM, VM, SM, VM, VM, VM, VM],
        [entries, (VM, f32(count, LANES)), rows_shape, (VM, f32(1, count)), send, send, halo, halo],
    )(prev, prev, own, stiff_table, field, own_entry, own_stiff, own_stiff_line)

    for sweep in range(ITERS):
        got_x = exchange(send_x, "sec", near)
        got_z = exchange(send_z, "sec", far)
        got_a = exchange(halo_a, "tile", near_tile)
        got_b = exchange(halo_b, "tile", far_tile)
        if sweep == 0:
            same, weight, factor = call(
                "setup",
                functools.partial(setup_kernel, chunks),
                [SM, VM, VM, HBM],
                [(VM, jax.ShapeDtypeStruct((total, count), jnp.bfloat16)), wide, wide],
                scratch_shapes=[
                    pltpu.VMEM((blocks, LANES), jnp.float32),
                    pltpu.VMEM((total, LANES), jnp.float32),
                    pltpu.VMEM((total, LANES), jnp.float32),
                    pltpu.SemaphoreType.DMA,
                ],
            )(rows, rows, stiff_line, tiled(spring[0]))
            (nearby,) = call("inner", functools.partial(inner_kernel, chunks), [VM], [big])(field)
        else:
            field, nearby = call(
                "inner",
                functools.partial(scatter_inner_kernel, chunks),
                [SM, VM, VM],
                [big, big],
                input_output_aliases={2: 0},
            )(rows, entry, nearby)
        nearby, base = call(
            "edge",
            functools.partial(edge_kernel, chunks),
            [SM] + [VM] * 9,
            [big, entries],
            input_output_aliases={9: 0},
        )(rows, field, entry, got_a, got_b, same, stiff, weight, factor, nearby)
        if sweep < ITERS - 1:
            entry, send_x, send_z, halo_a, halo_b = call(
                "step", functools.partial(step_kernel, chunks), [VM] * 6, [entries, send, send, halo, halo]
            )(got_x, got_z, base, same, factor, stiff)
    _, out = call(
        "last",
        last_kernel,
        [SM] + [VM] * 6,
        [big, (HBM, f32(fields, blocks, LANES))],
        scratch_shapes=[pltpu.VMEM((fields, total, LANES), jnp.float32), pltpu.SemaphoreType.DMA((2,))],
        input_output_aliases={1: 0},
    )(rows, nearby, got_x, got_z, base, same, factor)
    return untiled(out)[:, None]


def solution(mesh):
    placed = (
        P(None, "sec", "tile", None),
        P("sec", "tile", None),
        P(),
        P(None, "sec", "tile"),
        P("sec", "tile"),
    )
    return jax.shard_map(
        on_device,
        mesh=mesh,
        in_specs=placed,
        out_specs=P(None, "sec", "tile", None),
        check_vma=False,
    )
```

```python
import functools
import jax
import jax.numpy as jnp
from jax import lax
from jax.experimental import pallas as pl
from jax.experimental.pallas import tpu as pltpu
from jax.sharding import PartitionSpec as P

ITERS = 3
LOADS = 4
OWN_VMEM = 47
LANES = 128
SUB = 8

VM = pl.BlockSpec(memory_space=pltpu.VMEM)
SM = pl.BlockSpec(memory_space=pltpu.SMEM)
HBM = pl.BlockSpec(memory_space=pltpu.MemorySpace.HBM)


def f32(*shape):
    return jax.ShapeDtypeStruct(shape, jnp.float32)


def tile_row(block, chunks):
    row = block // chunks
    return (row // SUB) * (SUB * chunks) + (block % chunks) * SUB + row % SUB


def pieces(x):
    high = x.astype(jnp.bfloat16)
    low = (x - high.astype(jnp.float32)).astype(jnp.bfloat16)
    return high, low


def summed(same, x):
    high, low = pieces(x)
    return jnp.dot(same, high, preferred_element_type=jnp.float32) + jnp.dot(
        same, low, preferred_element_type=jnp.float32
    )


def parity(axis):
    return lax.axis_index(axis) % 2


def send_edges(entry, halo_a, halo_b, count, chunks):
    odd_tile = parity("tile")
    low = pl.multiple_of(count + (1 - odd_tile) * chunks, SUB)
    high = pl.multiple_of(count + odd_tile * chunks, SUB)
    halo_a[...] = entry[:, pl.ds(low, chunks), :]
    halo_b[...] = entry[:, pl.ds(high, chunks), :]


def columns(line):
    return jnp.concatenate(
        [
            jnp.broadcast_to(line[:, at : at + LANES], (LANES, LANES)).T
            for at in range(0, line.shape[1], LANES)
        ],
        axis=0,
    )


def each_slot(count, rows, body):
    def some(step, carry):
        for inner in range(8):
            slot = step * 8 + inner
            body(slot, rows(slot))
        return carry

    lax.fori_loop(0, count // 8, some, 0)


def into_smem(line, staged, scalars, sem):
    staged[...] = line.astype(jnp.int32)
    copy = pltpu.make_async_copy(staged, scalars, sem)
    copy.start()
    return copy


def load_parts(source, target, sem, pieces_each):
    rows = source.shape[1] // pieces_each
    copies = []
    for part in range(source.shape[0]):
        for piece in range(pieces_each):
            at = pl.ds(piece * rows, rows)
            copies.append(
                pltpu.make_async_copy(
                    source.at[part, at, :], target.at[part, at, :], sem.at[part * pieces_each + piece]
                )
            )
    return copies


def own_kernel(packed, displacement, field, entry, stiff, line, staged, scalars, sem, load_sem):
    loads = load_parts(displacement, field, load_sem, LOADS)
    for copy in loads:
        copy.start()
    listed = into_smem(packed[0:1, :], staged, scalars, sem)
    alive = lax.axis_index("sec") < lax.axis_size("sec") - 1
    line[...] = packed[2:3, :] * alive.astype(jnp.float32)
    stiff[...] = columns(line[...])
    listed.wait()
    for copy in loads:
        copy.wait()

    def take(slot, row):
        for part in range(2):
            entry[part, pl.ds(slot, 1), :] = field[part, pl.ds(row, 1), :]

    each_slot(packed.shape[1], lambda j: scalars[0, j], take)


def first_kernel(chunks, packed, prev, field, own_entry, own_stiff, own_stiff_line, entry, stiff, rows, stiff_line, send_x, send_z, halo_a, halo_b, staged, scalars, taken, sem):
    blocks = field.shape[1]
    matches = own_entry.shape[1]
    count = 2 * matches
    listed = into_smem(prev[1:2, :], staged, scalars, sem)
    even = parity("sec") == 0
    line = prev[2:3, :] * (lax.axis_index("sec") > 0).astype(jnp.float32)
    stiff_prev = columns(line)
    own_rows, prev_rows = packed[0:1, :].astype(jnp.int32), prev[1:2, :].astype(jnp.int32)
    for out, first, second in ((rows, own_rows, prev_rows), (stiff_line, own_stiff_line[...], line)):
        out[:, :matches] = jnp.where(even, first, second)
        out[:, matches:] = jnp.where(even, second, first)
    for part in range(2):
        for chunk in range(chunks):
            entry[part, pl.ds(count + chunk, 1), :] = field[part, pl.ds(chunk * SUB, 1), :]
            entry[part, pl.ds(count + chunks + chunk, 1), :] = field[
                part, pl.ds(blocks - SUB * chunks + chunk * SUB + SUB - 1, 1), :
            ]
    send_edges(entry, halo_a, halo_b, count, chunks)
    listed.wait()

    def take(slot, row):
        for part in range(2):
            taken[part, pl.ds(slot, 1), :] = field[part, pl.ds(row, 1), :]

    each_slot(matches, lambda j: scalars[0, j], take)

    def place(values, coupling, at, send):
        stiff[at : at + matches, :] = coupling
        for part in range(2):
            value = values[part]
            entry[part, at : at + matches, :] = value
            send[part] = value * coupling

    @pl.when(even)
    def _():
        place(own_entry, own_stiff[...], 0, send_x)
        place(taken, stiff_prev, matches, send_z)

    @pl.when(jnp.logical_not(even))
    def _():
        place(taken, stiff_prev, 0, send_x)
        place(own_entry, own_stiff[...], matches, send_z)


def setup_kernel(chunks, rows, rows_line, stiff_line, spring, same, weight, factor, picked, column):
    blocks = spring.shape[0]
    count = rows_line.shape[1]
    total = count + 2 * chunks
    last = blocks - SUB * chunks + SUB - 1
    column[:count, :] = columns(rows_line[...].astype(jnp.float32))
    edge = lax.broadcasted_iota(jnp.int32, (chunks, LANES), 0) * SUB
    column[count : count + chunks, :] = edge.astype(jnp.float32)
    column[count + chunks :, :] = (edge + last).astype(jnp.float32)
    place = lax.broadcasted_iota(jnp.int32, (1, LANES), 1)
    edge_line = jnp.where(place < chunks, place * SUB, (place - chunks) * SUB + last)
    edge_line = jnp.where(place < 2 * chunks, edge_line, -1).astype(jnp.float32)

    def band(step, carry):
        at = pl.ds(pl.multiple_of(step * 32, 32), 32)
        col = column[at, :]
        total_stiff = jnp.zeros((32, LANES), jnp.float32)
        for piece in range(count // LANES):
            cut = slice(piece * LANES, (piece + 1) * LANES)
            equal = col == rows_line[:, cut].astype(jnp.float32)
            same[at, cut] = equal.astype(jnp.float32).astype(jnp.bfloat16)
            total_stiff += jnp.where(equal, stiff_line[:, cut], 0.0)
        same[at, count:] = (col == edge_line).astype(jnp.float32).astype(jnp.bfloat16)
        factor[at, :] = jnp.broadcast_to(jnp.sum(total_stiff, axis=1, keepdims=True), (32, LANES))
        return carry

    lax.fori_loop(0, total // 32, band, 0)

    def take(slot, row):
        picked[pl.ds(slot, 1), :] = spring[pl.ds(row, 1), :]

    each_slot(count, lambda j: rows[0, j], take)
    for chunk in range(chunks):
        take(count + chunk, chunk * SUB)
        take(count + chunks + chunk, chunk * SUB + last)
    spring_here = picked[...]
    inverse = 1.0 / (4.0 * spring_here + factor[...])
    weight[...] = 4.0 * spring_here * inverse
    factor[...] = 0.8 * inverse


def stencil(field, nearby, start, chunks, top=False, bottom=False):
    span = SUB * chunks
    lane = lax.broadcasted_iota(jnp.int32, (SUB, LANES), 1)
    sub = lax.broadcasted_iota(jnp.int32, (SUB, LANES), 0)
    for part in range(2):

        def at(offset):
            return field[part, pl.ds(start + offset, SUB), :]

        before = jnp.zeros((SUB, LANES), jnp.float32)
        here = at(0)
        for chunk in range(chunks):
            offset = chunk * SUB
            after = at(offset + SUB) if chunk < chunks - 1 else jnp.zeros((SUB, LANES), jnp.float32)
            if top:
                up = jnp.where(sub == 0, 0.0, pltpu.roll(here, 1, 0))
            else:
                up = jnp.where(sub == 0, at(offset - span + SUB - 1), at(offset - 1))
            if bottom:
                down = jnp.where(sub == SUB - 1, 0.0, pltpu.roll(here, SUB - 1, 0))
            else:
                down = jnp.where(sub == SUB - 1, at(offset + span - SUB + 1), at(offset + 1))
            left = pltpu.roll(jnp.where(lane == LANES - 1, before, here), 1, 1)
            right = pltpu.roll(jnp.where(lane == 0, after, here), LANES - 1, 1)
            nearby[part, pl.ds(start + offset, SUB), :] = 0.2 * (((up + down) + (left + right)) + here)
            before, here = here, after


def bulk(chunks, rows, field, entry, same, stiff, weight, factor, nearby, base):
    blocks = field.shape[1]
    span = SUB * chunks
    strips = blocks // span
    count = rows.shape[1]
    stencil(field, nearby, 0, chunks, top=True)
    stencil(field, nearby, blocks - span, chunks, bottom=True)

    def pair(step, carry):
        for inner in range(2):
            stencil(field, nearby, pl.multiple_of((1 + step * 2 + inner) * span, SUB), chunks)
        return carry

    lax.fori_loop(0, (strips - 2) // 2, pair, 0)

    def take(slot, row):
        for part in range(2):
            base[part, pl.ds(slot, 1), :] = nearby[part, pl.ds(row, 1), :]

    each_slot(count, lambda j: rows[0, j], take)
    for chunk in range(chunks):
        take(count + chunk, chunk * SUB)
        take(count + chunks + chunk, blocks - span + chunk * SUB + SUB - 1)
    own = jnp.concatenate([entry[part, :count, :] * stiff[...] for part in range(2)], axis=1)
    total = summed(same[:, :count], own)
    for part in range(2):
        value = entry[part]
        base[part] = (
            value
            + weight[...] * (base[part] - value)
            - factor[...] * total[:, part * LANES : (part + 1) * LANES]
        )


def halo_rows(got_a, got_b):
    odd_tile = parity("tile") == 1
    return [
        (
            0.2 * jnp.where(odd_tile, got_a[part], got_b[part]),
            0.2 * jnp.where(odd_tile, got_b[part], got_a[part]),
        )
        for part in range(2)
    ]


def add_halo(field, halos, chunks):
    last = field.shape[1] - SUB * chunks + SUB - 1
    for part, (above, below) in enumerate(halos):
        for chunk in range(chunks):
            for start, halo in ((0, above), (last, below)):
                at = pl.ds(start + chunk * SUB, 1)
                field[part, at, :] = field[part, at, :] + halo[chunk : chunk + 1, :]


def inner_kernel(chunks, rows, entry, same, stiff, weight, factor, field, nearby, base):
    bulk(chunks, rows, field, entry, same, stiff, weight, factor, nearby, base)


def scatter_inner_kernel(chunks, rows, entry, same, stiff, weight, factor, got_a, got_b, stale, field, nearby, base):
    add_halo(field, halo_rows(got_a, got_b), chunks)

    def put(slot, row):
        for part in range(2):
            field[part, pl.ds(row, 1), :] = entry[part, pl.ds(slot, 1), :]

    each_slot(rows.shape[1], lambda j: rows[0, j], put)
    bulk(chunks, rows, field, entry, same, stiff, weight, factor, nearby, base)


def new_entries(got_x, got_z, halos, base, same, weight, factor):
    count = 2 * got_x.shape[1]
    got = jnp.concatenate(
        [jnp.concatenate([got_x[part], got_z[part]], axis=0) for part in range(2)], axis=1
    )
    unused = same.shape[1] - count - 2 * halos[0][0].shape[0]
    edges = jnp.concatenate(
        [
            jnp.concatenate([above, below, jnp.zeros((unused, LANES), jnp.float32)], axis=0)
            for above, below in halos
        ],
        axis=1,
    )
    total = summed(same[:, :count], got)
    outside = summed(same[:, count:], edges)
    out = []
    for part in range(2):
        cut = slice(part * LANES, (part + 1) * LANES)
        out.append(base[part] + weight[...] * outside[:, cut] + factor[...] * total[:, cut])
    return out


def step_kernel(chunks, got_x, got_z, got_a, got_b, base, same, weight, factor, stiff, entry, send_x, send_z, halo_a, halo_b):
    matches = got_x.shape[1]
    count = 2 * matches
    halos = halo_rows(got_a, got_b)
    for part, value in enumerate(new_entries(got_x, got_z, halos, base, same, weight, factor)):
        entry[part] = value
        send_x[part] = value[:matches] * stiff[:matches, :]
        send_z[part] = value[matches:count] * stiff[matches:, :]
    send_edges(entry, halo_a, halo_b, count, chunks)


def last_kernel(chunks, rows, stale, got_x, got_z, got_a, got_b, base, same, weight, factor, nearby, out, entry, sem):
    halos = halo_rows(got_a, got_b)
    add_halo(nearby, halos, chunks)
    for part, value in enumerate(new_entries(got_x, got_z, halos, base, same, weight, factor)):
        entry[part] = value
    stores = load_parts(nearby, out, sem, LOADS)
    for part in range(2):

        def put(slot, row):
            nearby[part, pl.ds(row, 1), :] = entry[part, pl.ds(slot, 1), :]

        each_slot(rows.shape[1], lambda j: rows[0, j], put)
        for copy in stores[part * LOADS : (part + 1) * LOADS]:
            copy.start()
    for copy in stores:
        copy.wait()


def exchange(array, axis, pairs):
    return lax.ppermute(array, axis, pairs)


def pairs_from(first, size):
    out = []
    for i in range(first, size - 1, 2):
        out += [(i, i + 1), (i + 1, i)]
    return out


def on_device(displacement, spring, stiff_table, match_blocks, match_class):
    fields, single, height, breadth = displacement.shape
    chunks = breadth // LANES
    blocks = height * chunks
    matches = match_blocks.shape[2]
    count = 2 * matches
    total = count + 2 * chunks
    sections, tiles = lax.axis_size("sec"), lax.axis_size("tile")
    near, far = pairs_from(0, sections), pairs_from(1, sections)
    near_tile, far_tile = pairs_from(0, tiles), pairs_from(1, tiles)

    def tiled(x):
        lead = x.shape[:-2]
        x = x.reshape(lead + (height // SUB, SUB, chunks, LANES))
        return jnp.swapaxes(x, -3, -2).reshape(lead + (blocks, LANES))

    def untiled(x):
        lead = x.shape[:-2]
        x = x.reshape(lead + (height // SUB, chunks, SUB, LANES))
        return jnp.swapaxes(x, -3, -2).reshape(lead + (height, breadth))

    def call(name, kernel, ins, outs, vmem=24 << 20, **more):
        return pl.pallas_call(
            kernel,
            in_specs=ins,
            out_specs=tuple(spec for spec, _ in outs),
            out_shape=tuple(shape for _, shape in outs),
            compiler_params=pltpu.CompilerParams(vmem_limit_bytes=vmem),
            name=name,
            **more,
        )

    halo = (VM, f32(fields, chunks, LANES))
    send = (VM, f32(fields, matches, LANES))
    entries = (VM, f32(fields, total, LANES))
    big = (VM, f32(fields, blocks, LANES))
    wide = (VM, f32(total, LANES))
    rows_shape = (VM, jax.ShapeDtypeStruct((1, count), jnp.int32))

    level = jnp.arange(stiff_table.shape[0], dtype=jnp.int32)[:, None]
    coupling = jnp.sum(jnp.where(match_class == level, stiff_table[:, None], 0.0), axis=0, keepdims=True)
    places = tile_row(match_blocks[:, 0], chunks).astype(jnp.float32)
    packed = jnp.concatenate([places, coupling], axis=0)
    prev = exchange(packed, "sec", [(i, i + 1) for i in range(sections - 1)])
    staging = [
        pltpu.VMEM((1, matches), jnp.int32),
        pltpu.SMEM((1, matches), jnp.int32),
    ]
    field, own_entry, own_stiff, own_stiff_line = call(
        "own",
        own_kernel,
        [VM, HBM],
        [big, send, (VM, f32(matches, LANES)), (VM, f32(1, matches))],
        scratch_shapes=staging + [pltpu.SemaphoreType.DMA, pltpu.SemaphoreType.DMA((2 * LOADS,))],
        vmem=OWN_VMEM << 20,
    )(packed, tiled(displacement[:, 0]))
    entry, stiff, rows, stiff_line, send_x, send_z, halo_a, halo_b = call(
        "first",
        functools.partial(first_kernel, chunks),
        [VM] * 6,
        [entries, (VM, f32(count, LANES)), rows_shape, (VM, f32(1, count)), send, send, halo, halo],
        scratch_shapes=staging
        + [pltpu.VMEM((fields, matches, LANES), jnp.float32), pltpu.SemaphoreType.DMA],
    )(packed, prev, field, own_entry, own_stiff, own_stiff_line)

    for sweep in range(ITERS):
        if sweep > 0:
            past = (got_a, got_b)
        got_x = exchange(send_x, "sec", near)
        got_z = exchange(send_z, "sec", far)
        got_a = exchange(halo_a, "tile", near_tile)
        got_b = exchange(halo_b, "tile", far_tile)
        if sweep == 0:
            same, weight, factor = call(
                "setup",
                functools.partial(setup_kernel, chunks),
                [SM, VM, VM, VM],
                [(VM, jax.ShapeDtypeStruct((total, count + LANES), jnp.bfloat16)), wide, wide],
                scratch_shapes=[pltpu.VMEM((total, LANES), jnp.float32)] * 2,
            )(rows, rows, stiff_line, tiled(spring[0]))
            nearby, base = call(
                "inner", functools.partial(inner_kernel, chunks), [SM] + [VM] * 6, [big, entries]
            )(rows, entry, same, stiff, weight, factor, field)
        else:
            field, nearby, base = call(
                "inner",
                functools.partial(scatter_inner_kernel, chunks),
                [SM] + [VM] * 8,
                [big, big, entries],
                input_output_aliases={8: 0},
            )(rows, entry, same, stiff, weight, factor, *past, nearby)
        if sweep < ITERS - 1:
            entry, send_x, send_z, halo_a, halo_b = call(
                "step", functools.partial(step_kernel, chunks), [VM] * 9, [entries, send, send, halo, halo]
            )(got_x, got_z, got_a, got_b, base, same, weight, factor, stiff)
    _, out = call(
        "last",
        functools.partial(last_kernel, chunks),
        [SM] + [VM] * 9,
        [big, (HBM, f32(fields, blocks, LANES))],
        scratch_shapes=[
            pltpu.VMEM((fields, total, LANES), jnp.float32),
            pltpu.SemaphoreType.DMA((2 * LOADS,)),
        ],
        input_output_aliases={1: 0},
    )(rows, nearby, got_x, got_z, got_a, got_b, base, same, weight, factor)
    return untiled(out)[:, None]


def solution(mesh):
    placed = (
        P(None, "sec", "tile", None),
        P("sec", "tile", None),
        P(),
        P(None, "sec", "tile"),
        P("sec", "tile"),
    )
    return jax.shard_map(
        on_device,
        mesh=mesh,
        in_specs=placed,
        out_specs=P(None, "sec", "tile", None),
        check_vma=False,
    )
```

```python
import functools
import math
import jax
import jax.numpy as jnp
from jax import lax
from jax.experimental import pallas as pl
from jax.experimental.pallas import tpu as pltpu
from jax.sharding import PartitionSpec as P

ITERS = 3
LOADS = 4
GROUP = 2
OWN_VMEM = 47
LANES = 128
SUB = 8

VM = pl.BlockSpec(memory_space=pltpu.VMEM)
SM = pl.BlockSpec(memory_space=pltpu.SMEM)
HBM = pl.BlockSpec(memory_space=pltpu.MemorySpace.HBM)


def f32(*shape):
    return jax.ShapeDtypeStruct(shape, jnp.float32)


def tile_row(block, chunks):
    row = block // chunks
    return (row // SUB) * (SUB * chunks) + (block % chunks) * SUB + row % SUB


def pieces(x, count):
    out = []
    for _ in range(count):
        out.append(x.astype(jnp.bfloat16))
        x = x - out[-1].astype(jnp.float32)
    return out


def summed(same, x, count=2):
    out = None
    for piece in pieces(x, count):
        product = jnp.dot(same, piece, preferred_element_type=jnp.float32)
        out = product if out is None else out + product
    return out


def parity(axis):
    return lax.axis_index(axis) % 2


def send_edges(entry, halo_a, halo_b, count, chunks):
    odd_tile = parity("tile")
    low = pl.multiple_of(count + (1 - odd_tile) * chunks, SUB)
    high = pl.multiple_of(count + odd_tile * chunks, SUB)
    halo_a[...] = entry[:, pl.ds(low, chunks), :]
    halo_b[...] = entry[:, pl.ds(high, chunks), :]


def columns(line):
    return jnp.concatenate(
        [
            jnp.broadcast_to(line[:, at : at + LANES], (LANES, LANES)).T
            for at in range(0, line.shape[1], LANES)
        ],
        axis=0,
    )


def each_slot(count, rows, body):
    def some(step, carry):
        for inner in range(8):
            slot = step * 8 + inner
            body(slot, rows(slot))
        return carry

    lax.fori_loop(0, count // 8, some, 0)


def into_smem(line, staged, scalars, sem):
    staged[...] = line.astype(jnp.int32)
    copy = pltpu.make_async_copy(staged, scalars, sem)
    copy.start()
    return copy


def load_parts(source, target, sem, pieces_each):
    rows = source.shape[1] // pieces_each
    copies = []
    for part in range(source.shape[0]):
        for piece in range(pieces_each):
            at = pl.ds(piece * rows, rows)
            copies.append(
                pltpu.make_async_copy(
                    source.at[part, at, :], target.at[part, at, :], sem.at[part * pieces_each + piece]
                )
            )
    return copies


def own_kernel(packed, displacement, field, entry, stiff, staged, scalars, sem, load_sem):
    loads = load_parts(displacement, field, load_sem, LOADS)
    for copy in loads:
        copy.start()
    listed = into_smem(packed[0:1, :], staged, scalars, sem)
    alive = lax.axis_index("sec") < lax.axis_size("sec") - 1
    stiff[...] = columns(packed[2:3, :] * alive.astype(jnp.float32))
    listed.wait()
    for part in range(2):
        for copy in loads[part * LOADS : (part + 1) * LOADS]:
            copy.wait()

        def take(slot, row):
            entry[part, pl.ds(slot, 1), :] = field[part, pl.ds(row, 1), :]

        each_slot(packed.shape[1], lambda j: scalars[0, j], take)


def first_kernel(chunks, packed, prev, field, own_entry, own_stiff, entry, stiff, rows, send_x, send_z, halo_a, halo_b, staged, scalars, taken, sem):
    blocks = field.shape[1]
    matches = own_entry.shape[1]
    count = 2 * matches
    listed = into_smem(prev[1:2, :], staged, scalars, sem)
    even = parity("sec") == 0
    line = prev[2:3, :] * (lax.axis_index("sec") > 0).astype(jnp.float32)
    stiff_prev = columns(line)
    own_rows, prev_rows = packed[0:1, :].astype(jnp.int32), prev[1:2, :].astype(jnp.int32)
    rows[:, :matches] = jnp.where(even, own_rows, prev_rows)
    rows[:, matches:] = jnp.where(even, prev_rows, own_rows)
    for part in range(2):
        for chunk in range(chunks):
            entry[part, pl.ds(count + chunk, 1), :] = field[part, pl.ds(chunk * SUB, 1), :]
            entry[part, pl.ds(count + chunks + chunk, 1), :] = field[
                part, pl.ds(blocks - SUB * chunks + chunk * SUB + SUB - 1, 1), :
            ]
    send_edges(entry, halo_a, halo_b, count, chunks)
    listed.wait()

    def take(slot, row):
        for part in range(2):
            taken[part, pl.ds(slot, 1), :] = field[part, pl.ds(row, 1), :]

    each_slot(matches, lambda j: scalars[0, j], take)

    def place(values, coupling, at, send):
        stiff[at : at + matches, :] = coupling
        for part in range(2):
            value = values[part]
            entry[part, at : at + matches, :] = value
            send[part] = value * coupling

    @pl.when(even)
    def _():
        place(own_entry, own_stiff[...], 0, send_x)
        place(taken, stiff_prev, matches, send_z)

    @pl.when(jnp.logical_not(even))
    def _():
        place(taken, stiff_prev, 0, send_x)
        place(own_entry, own_stiff[...], matches, send_z)


def setup_kernel(chunks, rows, rows_line, stiff, spring, same, weight, factor, picked, column):
    blocks = spring.shape[0]
    count = rows_line.shape[1]
    total = count + 2 * chunks
    last = blocks - SUB * chunks + SUB - 1
    column[:count, :] = columns(rows_line[...].astype(jnp.float32))
    edge = lax.broadcasted_iota(jnp.int32, (chunks, LANES), 0) * SUB
    column[count : count + chunks, :] = edge.astype(jnp.float32)
    column[count + chunks :, :] = (edge + last).astype(jnp.float32)
    place = lax.broadcasted_iota(jnp.int32, (1, LANES), 1)
    edge_line = jnp.where(place < chunks, place * SUB, (place - chunks) * SUB + last)
    edge_line = jnp.where(place < 2 * chunks, edge_line, -1).astype(jnp.float32)

    def band(step, carry):
        at = pl.ds(pl.multiple_of(step * 32, 32), 32)
        col = column[at, :]
        for piece in range(count // LANES):
            cut = slice(piece * LANES, (piece + 1) * LANES)
            equal = col == rows_line[:, cut].astype(jnp.float32)
            same[at, cut] = equal.astype(jnp.float32).astype(jnp.bfloat16)
        same[at, count:] = (col == edge_line).astype(jnp.float32).astype(jnp.bfloat16)
        return carry

    lax.fori_loop(0, total // 32, band, 0)

    def take(slot, row):
        picked[pl.ds(slot, 1), :] = spring[pl.ds(row, 1), :]

    each_slot(count, lambda j: rows[0, j], take)
    for chunk in range(chunks):
        take(count + chunk, chunk * SUB)
        take(count + chunks + chunk, chunk * SUB + last)
    spring_here = picked[...]
    inverse = 1.0 / (4.0 * spring_here + summed(same[:, :count], stiff[...], 3))
    weight[...] = 4.0 * spring_here * inverse
    factor[...] = 0.8 * inverse


def stencil(field, nearby, start, chunks, top=False, bottom=False):
    span = SUB * chunks
    lane = lax.broadcasted_iota(jnp.int32, (SUB, LANES), 1)
    sub = lax.broadcasted_iota(jnp.int32, (SUB, LANES), 0)
    for part in range(2):

        def at(offset):
            return field[part, pl.ds(start + offset, SUB), :]

        before = jnp.zeros((SUB, LANES), jnp.float32)
        here = at(0)
        for chunk in range(chunks):
            offset = chunk * SUB
            after = at(offset + SUB) if chunk < chunks - 1 else jnp.zeros((SUB, LANES), jnp.float32)
            if top:
                up = jnp.where(sub == 0, 0.0, pltpu.roll(here, 1, 0))
            else:
                up = jnp.where(sub == 0, at(offset - span + SUB - 1), at(offset - 1))
            if bottom:
                down = jnp.where(sub == SUB - 1, 0.0, pltpu.roll(here, SUB - 1, 0))
            else:
                down = jnp.where(sub == SUB - 1, at(offset + span - SUB + 1), at(offset + 1))
            left = pltpu.roll(jnp.where(lane == LANES - 1, before, here), 1, 1)
            right = pltpu.roll(jnp.where(lane == 0, after, here), LANES - 1, 1)
            nearby[part, pl.ds(start + offset, SUB), :] = 0.2 * (((up + down) + (left + right)) + here)
            before, here = here, after


def bulk(chunks, rows, field, nearby, base):
    blocks = field.shape[1]
    span = SUB * chunks
    strips = blocks // span
    count = rows.shape[1]
    stencil(field, nearby, 0, chunks, top=True)
    stencil(field, nearby, blocks - span, chunks, bottom=True)

    group = math.gcd(strips - 2, GROUP)

    def some(step, carry):
        for inner in range(group):
            stencil(field, nearby, pl.multiple_of((1 + step * group + inner) * span, SUB), chunks)
        return carry

    lax.fori_loop(0, (strips - 2) // group, some, 0)

    def take(slot, row):
        for part in range(2):
            base[part, pl.ds(slot, 1), :] = nearby[part, pl.ds(row, 1), :]

    each_slot(count, lambda j: rows[0, j], take)
    for chunk in range(chunks):
        take(count + chunk, chunk * SUB)
        take(count + chunks + chunk, blocks - span + chunk * SUB + SUB - 1)


def halo_rows(got_a, got_b):
    odd_tile = parity("tile") == 1
    return [
        (
            0.2 * jnp.where(odd_tile, got_a[part], got_b[part]),
            0.2 * jnp.where(odd_tile, got_b[part], got_a[part]),
        )
        for part in range(2)
    ]


def add_halo(field, halos, chunks):
    last = field.shape[1] - SUB * chunks + SUB - 1
    for part, (above, below) in enumerate(halos):
        for chunk in range(chunks):
            for start, halo in ((0, above), (last, below)):
                at = pl.ds(start + chunk * SUB, 1)
                field[part, at, :] = field[part, at, :] + halo[chunk : chunk + 1, :]


def inner_kernel(chunks, rows, field, nearby, base):
    bulk(chunks, rows, field, nearby, base)


def scatter_inner_kernel(chunks, rows, entry, got_a, got_b, stale, field, nearby, base):
    add_halo(field, halo_rows(got_a, got_b), chunks)

    def put(slot, row):
        for part in range(2):
            field[part, pl.ds(row, 1), :] = entry[part, pl.ds(slot, 1), :]

    each_slot(rows.shape[1], lambda j: rows[0, j], put)
    bulk(chunks, rows, field, nearby, base)


def new_entries(got_x, got_z, halos, entry, base, same, weight, factor, stiff):
    matches = got_x.shape[1]
    count = 2 * matches
    term = jnp.concatenate(
        [
            jnp.concatenate(
                [
                    got[part] - stiff[at : at + matches, :] * entry[part, at : at + matches, :]
                    for at, got in ((0, got_x), (matches, got_z))
                ],
                axis=0,
            )
            for part in range(2)
        ],
        axis=1,
    )
    unused = same.shape[1] - count - 2 * halos[0][0].shape[0]
    edges = jnp.concatenate(
        [
            jnp.concatenate([above, below, jnp.zeros((unused, LANES), jnp.float32)], axis=0)
            for above, below in halos
        ],
        axis=1,
    )
    total = summed(same[:, :count], term)
    outside = summed(same[:, count:], edges)
    out = []
    for part in range(2):
        cut = slice(part * LANES, (part + 1) * LANES)
        value = entry[part]
        out.append(
            value
            + weight[...] * ((base[part] - value) + outside[:, cut])
            + factor[...] * total[:, cut]
        )
    return out


def step_kernel(chunks, got_x, got_z, got_a, got_b, old, base, same, weight, factor, stiff, entry, send_x, send_z, halo_a, halo_b):
    matches = got_x.shape[1]
    count = 2 * matches
    halos = halo_rows(got_a, got_b)
    for part, value in enumerate(new_entries(got_x, got_z, halos, old, base, same, weight, factor, stiff)):
        entry[part] = value
        send_x[part] = value[:matches] * stiff[:matches, :]
        send_z[part] = value[matches:count] * stiff[matches:, :]
    send_edges(entry, halo_a, halo_b, count, chunks)


def last_kernel(chunks, rows, stale, got_x, got_z, got_a, got_b, old, base, same, weight, factor, stiff, nearby, out, entry, sem):
    halos = halo_rows(got_a, got_b)
    add_halo(nearby, halos, chunks)
    for part, value in enumerate(new_entries(got_x, got_z, halos, old, base, same, weight, factor, stiff)):
        entry[part] = value
    stores = load_parts(nearby, out, sem, LOADS)
    for part in range(2):

        def put(slot, row):
            nearby[part, pl.ds(row, 1), :] = entry[part, pl.ds(slot, 1), :]

        each_slot(rows.shape[1], lambda j: rows[0, j], put)
        for copy in stores[part * LOADS : (part + 1) * LOADS]:
            copy.start()
    for copy in stores:
        copy.wait()


def exchange(array, axis, pairs):
    return lax.ppermute(array, axis, pairs)


def pairs_from(first, size):
    out = []
    for i in range(first, size - 1, 2):
        out += [(i, i + 1), (i + 1, i)]
    return out


def on_device(displacement, spring, stiff_table, match_blocks, match_class):
    fields, single, height, breadth = displacement.shape
    chunks = breadth // LANES
    blocks = height * chunks
    matches = match_blocks.shape[2]
    count = 2 * matches
    total = count + 2 * chunks
    sections, tiles = lax.axis_size("sec"), lax.axis_size("tile")
    near, far = pairs_from(0, sections), pairs_from(1, sections)
    near_tile, far_tile = pairs_from(0, tiles), pairs_from(1, tiles)

    def tiled(x):
        lead = x.shape[:-2]
        x = x.reshape(lead + (height // SUB, SUB, chunks, LANES))
        return jnp.swapaxes(x, -3, -2).reshape(lead + (blocks, LANES))

    def untiled(x):
        lead = x.shape[:-2]
        x = x.reshape(lead + (height // SUB, chunks, SUB, LANES))
        return jnp.swapaxes(x, -3, -2).reshape(lead + (height, breadth))

    def call(name, kernel, ins, outs, vmem=24 << 20, **more):
        return pl.pallas_call(
            kernel,
            in_specs=ins,
            out_specs=tuple(spec for spec, _ in outs),
            out_shape=tuple(shape for _, shape in outs),
            compiler_params=pltpu.CompilerParams(vmem_limit_bytes=vmem),
            name=name,
            **more,
        )

    halo = (VM, f32(fields, chunks, LANES))
    send = (VM, f32(fields, matches, LANES))
    entries = (VM, f32(fields, total, LANES))
    big = (VM, f32(fields, blocks, LANES))
    wide = (VM, f32(total, LANES))
    rows_shape = (VM, jax.ShapeDtypeStruct((1, count), jnp.int32))

    level = jnp.arange(stiff_table.shape[0], dtype=jnp.int32)[:, None]
    coupling = jnp.sum(jnp.where(match_class == level, stiff_table[:, None], 0.0), axis=0, keepdims=True)
    places = tile_row(match_blocks[:, 0], chunks).astype(jnp.float32)
    packed = jnp.concatenate([places, coupling], axis=0)
    prev = exchange(packed, "sec", [(i, i + 1) for i in range(sections - 1)])
    staging = [
        pltpu.VMEM((1, matches), jnp.int32),
        pltpu.SMEM((1, matches), jnp.int32),
    ]
    field, own_entry, own_stiff = call(
        "own",
        own_kernel,
        [VM, HBM],
        [big, send, (VM, f32(matches, LANES))],
        scratch_shapes=staging + [pltpu.SemaphoreType.DMA, pltpu.SemaphoreType.DMA((2 * LOADS,))],
        vmem=OWN_VMEM << 20,
    )(packed, tiled(displacement[:, 0]))
    entry, stiff, rows, send_x, send_z, halo_a, halo_b = call(
        "first",
        functools.partial(first_kernel, chunks),
        [VM] * 5,
        [entries, (VM, f32(count, LANES)), rows_shape, send, send, halo, halo],
        scratch_shapes=staging
        + [pltpu.VMEM((fields, matches, LANES), jnp.float32), pltpu.SemaphoreType.DMA],
    )(packed, prev, field, own_entry, own_stiff)

    for sweep in range(ITERS):
        if sweep > 0:
            past = (got_a, got_b)
        got_x = exchange(send_x, "sec", near)
        got_z = exchange(send_z, "sec", far)
        got_a = exchange(halo_a, "tile", near_tile)
        got_b = exchange(halo_b, "tile", far_tile)
        if sweep == 0:
            same, weight, factor = call(
                "setup",
                functools.partial(setup_kernel, chunks),
                [SM, VM, VM, VM],
                [(VM, jax.ShapeDtypeStruct((total, count + LANES), jnp.bfloat16)), wide, wide],
                scratch_shapes=[pltpu.VMEM((total, LANES), jnp.float32)] * 2,
            )(rows, rows, stiff, tiled(spring[0]))
            nearby, base = call(
                "inner", functools.partial(inner_kernel, chunks), [SM, VM], [big, entries]
            )(rows, field)
        else:
            field, nearby, base = call(
                "inner",
                functools.partial(scatter_inner_kernel, chunks),
                [SM] + [VM] * 4,
                [big, big, entries],
                input_output_aliases={4: 0},
            )(rows, entry, *past, nearby)
        if sweep < ITERS - 1:
            entry, send_x, send_z, halo_a, halo_b = call(
                "step", functools.partial(step_kernel, chunks), [VM] * 10, [entries, send, send, halo, halo]
            )(got_x, got_z, got_a, got_b, entry, base, same, weight, factor, stiff)
    _, out = call(
        "last",
        functools.partial(last_kernel, chunks),
        [SM] + [VM] * 11,
        [big, (HBM, f32(fields, blocks, LANES))],
        scratch_shapes=[
            pltpu.VMEM((fields, total, LANES), jnp.float32),
            pltpu.SemaphoreType.DMA((2 * LOADS,)),
        ],
        input_output_aliases={1: 0},
    )(rows, nearby, got_x, got_z, got_a, got_b, entry, base, same, weight, factor, stiff)
    return untiled(out)[:, None]


def solution(mesh):
    placed = (
        P(None, "sec", "tile", None),
        P("sec", "tile", None),
        P(),
        P(None, "sec", "tile"),
        P("sec", "tile"),
    )
    return jax.shard_map(
        on_device,
        mesh=mesh,
        in_specs=placed,
        out_specs=P(None, "sec", "tile", None),
        check_vma=False,
    )
```

```python
import functools
import math
import jax
import jax.numpy as jnp
from jax import lax
from jax.experimental import pallas as pl
from jax.experimental.pallas import tpu as pltpu
from jax.sharding import PartitionSpec as P

ITERS = 3
LOADS = 4
GROUP = 2
OWN_VMEM = 47
LANES = 128
SUB = 8

VM = pl.BlockSpec(memory_space=pltpu.VMEM)
SM = pl.BlockSpec(memory_space=pltpu.SMEM)
HBM = pl.BlockSpec(memory_space=pltpu.MemorySpace.HBM)


def f32(*shape):
    return jax.ShapeDtypeStruct(shape, jnp.float32)


def tile_row(block, chunks):
    bits, low = chunks.bit_length() - 1, SUB.bit_length() - 1
    row = block >> bits
    return ((row >> low) << (bits + low)) | ((block & (chunks - 1)) << low) | (row & (SUB - 1))


def pieces(x, count):
    out = []
    for _ in range(count):
        out.append(x.astype(jnp.bfloat16))
        x = x - out[-1].astype(jnp.float32)
    return out


def summed(same, x, count=2):
    out = None
    for piece in pieces(x, count):
        product = jnp.dot(same, piece, preferred_element_type=jnp.float32)
        out = product if out is None else out + product
    return out


def parity(axis):
    return lax.axis_index(axis) % 2


def send_edges(entry, halo_a, halo_b, count, chunks):
    odd_tile = parity("tile")
    low = pl.multiple_of(count + (1 - odd_tile) * chunks, SUB)
    high = pl.multiple_of(count + odd_tile * chunks, SUB)
    halo_a[...] = entry[:, pl.ds(low, chunks), :]
    halo_b[...] = entry[:, pl.ds(high, chunks), :]


def columns(line):
    return jnp.concatenate(
        [
            jnp.broadcast_to(line[:, at : at + LANES], (LANES, LANES)).T
            for at in range(0, line.shape[1], LANES)
        ],
        axis=0,
    )


def each_slot(count, rows, body):
    def some(step, carry):
        for inner in range(16):
            slot = step * 16 + inner
            body(slot, rows(slot))
        return carry

    lax.fori_loop(0, count // 16, some, 0)


def into_smem(line, staged, scalars, sem):
    staged[...] = line
    copy = pltpu.make_async_copy(staged, scalars, sem)
    copy.start()
    return copy


def load_parts(source, target, sem, pieces_each):
    rows = source.shape[1] // pieces_each
    copies = []
    for part in range(source.shape[0]):
        for piece in range(pieces_each):
            at = pl.ds(piece * rows, rows)
            copies.append(
                pltpu.make_async_copy(
                    source.at[part, at, :], target.at[part, at, :], sem.at[part * pieces_each + piece]
                )
            )
    return copies


def coupling_of(classes, table, alive):
    out = jnp.zeros(classes.shape, jnp.float32)
    for level in range(table.shape[1]):
        out = jnp.where(classes == level, table[:, level : level + 1], out)
    return out * alive.astype(jnp.float32)


def own_kernel(chunks, packed, displacement, field, entry, staged, scalars, sem, load_sem):
    loads = load_parts(displacement, field, load_sem, LOADS)
    for copy in loads:
        copy.start()
    listed = into_smem(tile_row(packed[0], chunks), staged, scalars, sem)
    listed.wait()
    for part in range(2):
        for copy in loads[part * LOADS : (part + 1) * LOADS]:
            copy.wait()

        def take(slot, row):
            entry[part, pl.ds(slot, 1), :] = field[part, pl.ds(row, 1), :]

        each_slot(packed.shape[2], lambda j: scalars[0, j], take)


def first_kernel(chunks, table, packed, prev, field, own_entry, entry, stiff, rows, send_x, send_z, halo_a, halo_b, staged, scalars, taken, sem):
    blocks = field.shape[1]
    matches = own_entry.shape[1]
    count = 2 * matches
    own_rows, prev_rows = tile_row(packed[0], chunks), tile_row(prev[1], chunks)
    listed = into_smem(prev_rows, staged, scalars, sem)
    even = parity("sec") == 0
    section = lax.axis_index("sec")
    stiff_own = columns(coupling_of(packed[2], table, section < lax.axis_size("sec") - 1))
    stiff_prev = columns(coupling_of(prev[2], table, section > 0))
    rows[:, :matches] = jnp.where(even, own_rows, prev_rows)
    rows[:, matches:] = jnp.where(even, prev_rows, own_rows)
    for part in range(2):
        for chunk in range(chunks):
            entry[part, pl.ds(count + chunk, 1), :] = field[part, pl.ds(chunk * SUB, 1), :]
            entry[part, pl.ds(count + chunks + chunk, 1), :] = field[
                part, pl.ds(blocks - SUB * chunks + chunk * SUB + SUB - 1, 1), :
            ]
    send_edges(entry, halo_a, halo_b, count, chunks)
    listed.wait()

    def take(slot, row):
        for part in range(2):
            taken[part, pl.ds(slot, 1), :] = field[part, pl.ds(row, 1), :]

    each_slot(matches, lambda j: scalars[0, j], take)

    def place(values, coupling, at, send):
        stiff[at : at + matches, :] = coupling
        for part in range(2):
            value = values[part]
            entry[part, at : at + matches, :] = value
            send[part] = value * coupling

    @pl.when(even)
    def _():
        place(own_entry, stiff_own, 0, send_x)
        place(taken, stiff_prev, matches, send_z)

    @pl.when(jnp.logical_not(even))
    def _():
        place(taken, stiff_prev, 0, send_x)
        place(own_entry, stiff_own, matches, send_z)


def setup_kernel(chunks, rows, rows_line, stiff, spring, same, weight, factor, picked, column):
    blocks = spring.shape[0]
    count = rows_line.shape[1]
    total = count + 2 * chunks
    last = blocks - SUB * chunks + SUB - 1
    column[:count, :] = columns(rows_line[...].astype(jnp.float32))
    edge = lax.broadcasted_iota(jnp.int32, (chunks, LANES), 0) * SUB
    column[count : count + chunks, :] = edge.astype(jnp.float32)
    column[count + chunks :, :] = (edge + last).astype(jnp.float32)
    place = lax.broadcasted_iota(jnp.int32, (1, LANES), 1)
    edge_line = jnp.where(place < chunks, place * SUB, (place - chunks) * SUB + last)
    edge_line = jnp.where(place < 2 * chunks, edge_line, -1).astype(jnp.float32)

    def band(step, carry):
        at = pl.ds(pl.multiple_of(step * 32, 32), 32)
        col = column[at, :]
        for piece in range(count // LANES):
            cut = slice(piece * LANES, (piece + 1) * LANES)
            equal = col == rows_line[:, cut].astype(jnp.float32)
            same[at, cut] = equal.astype(jnp.float32).astype(jnp.bfloat16)
        same[at, count:] = (col == edge_line).astype(jnp.float32).astype(jnp.bfloat16)
        return carry

    lax.fori_loop(0, total // 32, band, 0)

    def take(slot, row):
        picked[pl.ds(slot, 1), :] = spring[pl.ds(row, 1), :]

    each_slot(count, lambda j: rows[0, j], take)
    for chunk in range(chunks):
        take(count + chunk, chunk * SUB)
        take(count + chunks + chunk, chunk * SUB + last)
    spring_here = picked[...]
    inverse = 1.0 / (4.0 * spring_here + summed(same[:, :count], stiff[...], 3))
    weight[...] = 4.0 * spring_here * inverse
    factor[...] = 0.8 * inverse


def stencil(field, nearby, start, chunks, top=False, bottom=False):
    span = SUB * chunks
    lane = lax.broadcasted_iota(jnp.int32, (SUB, LANES), 1)
    sub = lax.broadcasted_iota(jnp.int32, (SUB, LANES), 0)
    for part in range(2):

        def at(offset):
            return field[part, pl.ds(start + offset, SUB), :]

        before = jnp.zeros((SUB, LANES), jnp.float32)
        here = at(0)
        for chunk in range(chunks):
            offset = chunk * SUB
            after = at(offset + SUB) if chunk < chunks - 1 else jnp.zeros((SUB, LANES), jnp.float32)
            if top:
                up = jnp.where(sub == 0, 0.0, pltpu.roll(here, 1, 0))
            else:
                up = jnp.where(sub == 0, at(offset - span + SUB - 1), at(offset - 1))
            if bottom:
                down = jnp.where(sub == SUB - 1, 0.0, pltpu.roll(here, SUB - 1, 0))
            else:
                down = jnp.where(sub == SUB - 1, at(offset + span - SUB + 1), at(offset + 1))
            left = pltpu.roll(jnp.where(lane == LANES - 1, before, here), 1, 1)
            right = pltpu.roll(jnp.where(lane == 0, after, here), LANES - 1, 1)
            nearby[part, pl.ds(start + offset, SUB), :] = 0.2 * (((up + down) + (left + right)) + here)
            before, here = here, after


def bulk(chunks, rows, field, nearby, base):
    blocks = field.shape[1]
    span = SUB * chunks
    strips = blocks // span
    count = rows.shape[1]
    stencil(field, nearby, 0, chunks, top=True)
    stencil(field, nearby, blocks - span, chunks, bottom=True)

    group = math.gcd(strips - 2, GROUP)

    def some(step, carry):
        for inner in range(group):
            stencil(field, nearby, pl.multiple_of((1 + step * group + inner) * span, SUB), chunks)
        return carry

    lax.fori_loop(0, (strips - 2) // group, some, 0)

    def take(slot, row):
        for part in range(2):
            base[part, pl.ds(slot, 1), :] = nearby[part, pl.ds(row, 1), :]

    each_slot(count, lambda j: rows[0, j], take)
    for chunk in range(chunks):
        take(count + chunk, chunk * SUB)
        take(count + chunks + chunk, blocks - span + chunk * SUB + SUB - 1)


def halo_rows(got_a, got_b):
    odd_tile = parity("tile") == 1
    return [
        (
            0.2 * jnp.where(odd_tile, got_a[part], got_b[part]),
            0.2 * jnp.where(odd_tile, got_b[part], got_a[part]),
        )
        for part in range(2)
    ]


def add_halo(field, halos, chunks):
    last = field.shape[1] - SUB * chunks + SUB - 1
    for part, (above, below) in enumerate(halos):
        for chunk in range(chunks):
            for start, halo in ((0, above), (last, below)):
                at = pl.ds(start + chunk * SUB, 1)
                field[part, at, :] = field[part, at, :] + halo[chunk : chunk + 1, :]


def inner_kernel(chunks, rows, field, nearby, base):
    bulk(chunks, rows, field, nearby, base)


def scatter_inner_kernel(chunks, rows, entry, got_a, got_b, stale, field, nearby, base):
    add_halo(field, halo_rows(got_a, got_b), chunks)

    def put(slot, row):
        for part in range(2):
            field[part, pl.ds(row, 1), :] = entry[part, pl.ds(slot, 1), :]

    each_slot(rows.shape[1], lambda j: rows[0, j], put)
    bulk(chunks, rows, field, nearby, base)


def new_entries(got_x, got_z, halos, entry, base, same, weight, factor, stiff):
    matches = got_x.shape[1]
    count = 2 * matches
    term = jnp.concatenate(
        [
            jnp.concatenate(
                [
                    got[part] - stiff[at : at + matches, :] * entry[part, at : at + matches, :]
                    for at, got in ((0, got_x), (matches, got_z))
                ],
                axis=0,
            )
            for part in range(2)
        ],
        axis=1,
    )
    unused = same.shape[1] - count - 2 * halos[0][0].shape[0]
    edges = jnp.concatenate(
        [
            jnp.concatenate([above, below, jnp.zeros((unused, LANES), jnp.float32)], axis=0)
            for above, below in halos
        ],
        axis=1,
    )
    total = summed(same[:, :count], term)
    outside = summed(same[:, count:], edges)
    out = []
    for part in range(2):
        cut = slice(part * LANES, (part + 1) * LANES)
        value = entry[part]
        out.append(
            value
            + weight[...] * ((base[part] - value) + outside[:, cut])
            + factor[...] * total[:, cut]
        )
    return out


def step_kernel(chunks, got_x, got_z, got_a, got_b, old, base, same, weight, factor, stiff, entry, send_x, send_z, halo_a, halo_b):
    matches = got_x.shape[1]
    count = 2 * matches
    halos = halo_rows(got_a, got_b)
    for part, value in enumerate(new_entries(got_x, got_z, halos, old, base, same, weight, factor, stiff)):
        entry[part] = value
        send_x[part] = value[:matches] * stiff[:matches, :]
        send_z[part] = value[matches:count] * stiff[matches:, :]
    send_edges(entry, halo_a, halo_b, count, chunks)


def last_kernel(chunks, rows, stale, got_x, got_z, got_a, got_b, old, base, same, weight, factor, stiff, nearby, out, entry, sem):
    halos = halo_rows(got_a, got_b)
    add_halo(nearby, halos, chunks)
    for part, value in enumerate(new_entries(got_x, got_z, halos, old, base, same, weight, factor, stiff)):
        entry[part] = value
    stores = load_parts(nearby, out, sem, LOADS)
    for part in range(2):

        def put(slot, row):
            nearby[part, pl.ds(row, 1), :] = entry[part, pl.ds(slot, 1), :]

        each_slot(rows.shape[1], lambda j: rows[0, j], put)
        for copy in stores[part * LOADS : (part + 1) * LOADS]:
            copy.start()
    for copy in stores:
        copy.wait()


def exchange(array, axis, pairs):
    return lax.ppermute(array, axis, pairs)


def pairs_from(first, size):
    out = []
    for i in range(first, size - 1, 2):
        out += [(i, i + 1), (i + 1, i)]
    return out


def on_device(displacement, spring, stiff_table, match_blocks, match_class):
    fields, single, height, breadth = displacement.shape
    chunks = breadth // LANES
    blocks = height * chunks
    matches = match_blocks.shape[2]
    count = 2 * matches
    total = count + 2 * chunks
    sections, tiles = lax.axis_size("sec"), lax.axis_size("tile")
    near, far = pairs_from(0, sections), pairs_from(1, sections)
    near_tile, far_tile = pairs_from(0, tiles), pairs_from(1, tiles)

    def tiled(x):
        lead = x.shape[:-2]
        x = x.reshape(lead + (height // SUB, SUB, chunks, LANES))
        return jnp.swapaxes(x, -3, -2).reshape(lead + (blocks, LANES))

    def untiled(x):
        lead = x.shape[:-2]
        x = x.reshape(lead + (height // SUB, chunks, SUB, LANES))
        return jnp.swapaxes(x, -3, -2).reshape(lead + (height, breadth))

    def call(name, kernel, ins, outs, vmem=24 << 20, **more):
        return pl.pallas_call(
            kernel,
            in_specs=ins,
            out_specs=tuple(spec for spec, _ in outs),
            out_shape=tuple(shape for _, shape in outs),
            compiler_params=pltpu.CompilerParams(vmem_limit_bytes=vmem),
            name=name,
            **more,
        )

    halo = (VM, f32(fields, chunks, LANES))
    send = (VM, f32(fields, matches, LANES))
    entries = (VM, f32(fields, total, LANES))
    big = (VM, f32(fields, blocks, LANES))
    wide = (VM, f32(total, LANES))
    rows_shape = (VM, jax.ShapeDtypeStruct((1, count), jnp.int32))

    packed = jnp.concatenate([match_blocks, match_class[:, None]], axis=0)
    prev = exchange(packed, "sec", [(i, i + 1) for i in range(sections - 1)])
    staging = [
        pltpu.VMEM((1, matches), jnp.int32),
        pltpu.SMEM((1, matches), jnp.int32),
    ]
    field, own_entry = call(
        "own",
        functools.partial(own_kernel, chunks),
        [VM, HBM],
        [big, send],
        scratch_shapes=staging + [pltpu.SemaphoreType.DMA, pltpu.SemaphoreType.DMA((2 * LOADS,))],
        vmem=OWN_VMEM << 20,
    )(packed, tiled(displacement[:, 0]))
    entry, stiff, rows, send_x, send_z, halo_a, halo_b = call(
        "first",
        functools.partial(first_kernel, chunks),
        [VM] * 5,
        [entries, (VM, f32(count, LANES)), rows_shape, send, send, halo, halo],
        scratch_shapes=staging
        + [pltpu.VMEM((fields, matches, LANES), jnp.float32), pltpu.SemaphoreType.DMA],
    )(stiff_table[None], packed, prev, field, own_entry)

    for sweep in range(ITERS):
        if sweep > 0:
            past = (got_a, got_b)
        got_x = exchange(send_x, "sec", near)
        got_z = exchange(send_z, "sec", far)
        got_a = exchange(halo_a, "tile", near_tile)
        got_b = exchange(halo_b, "tile", far_tile)
        if sweep == 0:
            same, weight, factor = call(
                "setup",
                functools.partial(setup_kernel, chunks),
                [SM, VM, VM, VM],
                [(VM, jax.ShapeDtypeStruct((total, count + LANES), jnp.bfloat16)), wide, wide],
                scratch_shapes=[pltpu.VMEM((total, LANES), jnp.float32)] * 2,
            )(rows, rows, stiff, tiled(spring[0]))
            nearby, base = call(
                "inner", functools.partial(inner_kernel, chunks), [SM, VM], [big, entries]
            )(rows, field)
        else:
            field, nearby, base = call(
                "inner",
                functools.partial(scatter_inner_kernel, chunks),
                [SM] + [VM] * 4,
                [big, big, entries],
                input_output_aliases={4: 0},
            )(rows, entry, *past, nearby)
        if sweep < ITERS - 1:
            entry, send_x, send_z, halo_a, halo_b = call(
                "step", functools.partial(step_kernel, chunks), [VM] * 10, [entries, send, send, halo, halo]
            )(got_x, got_z, got_a, got_b, entry, base, same, weight, factor, stiff)
    _, out = call(
        "last",
        functools.partial(last_kernel, chunks),
        [SM] + [VM] * 11,
        [big, (HBM, f32(fields, blocks, LANES))],
        scratch_shapes=[
            pltpu.VMEM((fields, total, LANES), jnp.float32),
            pltpu.SemaphoreType.DMA((2 * LOADS,)),
        ],
        input_output_aliases={1: 0},
    )(rows, nearby, got_x, got_z, got_a, got_b, entry, base, same, weight, factor, stiff)
    return untiled(out)[:, None]


def solution(mesh):
    placed = (
        P(None, "sec", "tile", None),
        P("sec", "tile", None),
        P(),
        P(None, "sec", "tile"),
        P("sec", "tile"),
    )
    return jax.shard_map(
        on_device,
        mesh=mesh,
        in_specs=placed,
        out_specs=P(None, "sec", "tile", None),
        check_vma=False,
    )
```

```python
import functools
import math
import jax
import jax.numpy as jnp
from jax import lax
from jax.experimental import pallas as pl
from jax.experimental.pallas import tpu as pltpu
from jax.sharding import PartitionSpec as P

ITERS = 3
LOADS = 4
GROUP = 6
OWN_VMEM = 47
LANES = 128
SUB = 8

VM = pl.BlockSpec(memory_space=pltpu.VMEM)
SM = pl.BlockSpec(memory_space=pltpu.SMEM)
HBM = pl.BlockSpec(memory_space=pltpu.MemorySpace.HBM)


def f32(*shape):
    return jax.ShapeDtypeStruct(shape, jnp.float32)


def tile_row(block, chunks):
    bits, low = chunks.bit_length() - 1, SUB.bit_length() - 1
    row = block >> bits
    return ((row >> low) << (bits + low)) | ((block & (chunks - 1)) << low) | (row & (SUB - 1))


def pieces(x, count):
    out = []
    for _ in range(count):
        out.append(x.astype(jnp.bfloat16))
        x = x - out[-1].astype(jnp.float32)
    return out


def summed(same, x, count=2):
    out = None
    for piece in pieces(x, count):
        product = jnp.dot(same, piece, preferred_element_type=jnp.float32)
        out = product if out is None else out + product
    return out


def parity(axis):
    return lax.axis_index(axis) % 2


def send_edges(entry, halo_a, halo_b, count, chunks):
    odd_tile = parity("tile")
    low = pl.multiple_of(count + (1 - odd_tile) * chunks, SUB)
    high = pl.multiple_of(count + odd_tile * chunks, SUB)
    halo_a[...] = entry[:, pl.ds(low, chunks), :]
    halo_b[...] = entry[:, pl.ds(high, chunks), :]


def columns(line):
    return jnp.concatenate(
        [
            jnp.broadcast_to(line[:, at : at + LANES], (LANES, LANES)).T
            for at in range(0, line.shape[1], LANES)
        ],
        axis=0,
    )


def each_slot(count, rows, body):
    def some(step, carry):
        for inner in range(16):
            slot = step * 16 + inner
            body(slot, rows(slot))
        return carry

    lax.fori_loop(0, count // 16, some, 0)


def into_smem(line, staged, scalars, sem):
    staged[...] = line
    copy = pltpu.make_async_copy(staged, scalars, sem)
    copy.start()
    return copy


def load_parts(source, target, sem, pieces_each):
    rows = source.shape[1] // pieces_each
    copies = []
    for part in range(source.shape[0]):
        for piece in range(pieces_each):
            at = pl.ds(piece * rows, rows)
            copies.append(
                pltpu.make_async_copy(
                    source.at[part, at, :], target.at[part, at, :], sem.at[part * pieces_each + piece]
                )
            )
    return copies


def coupling_of(classes, table, alive):
    out = jnp.zeros(classes.shape, jnp.float32)
    for level in range(table.shape[1]):
        out = jnp.where(classes == level, table[:, level : level + 1], out)
    return out * alive.astype(jnp.float32)


def own_kernel(chunks, packed, displacement, field, entry, staged, scalars, sem, load_sem):
    loads = load_parts(displacement, field, load_sem, LOADS)
    for copy in loads:
        copy.start()
    listed = into_smem(tile_row(packed[0], chunks), staged, scalars, sem)
    listed.wait()
    for part in range(2):
        for copy in loads[part * LOADS : (part + 1) * LOADS]:
            copy.wait()

        def take(slot, row):
            entry[part, pl.ds(slot, 1), :] = field[part, pl.ds(row, 1), :]

        each_slot(packed.shape[2], lambda j: scalars[0, j], take)


def first_kernel(chunks, table, packed, prev, field, own_entry, entry, stiff, rows, send_x, send_z, halo_a, halo_b, staged, scalars, taken, sem):
    blocks = field.shape[1]
    matches = own_entry.shape[1]
    count = 2 * matches
    own_rows, prev_rows = tile_row(packed[0], chunks), tile_row(prev[1], chunks)
    listed = into_smem(prev_rows, staged, scalars, sem)
    even = parity("sec") == 0
    section = lax.axis_index("sec")
    stiff_own = columns(coupling_of(packed[2], table, section < lax.axis_size("sec") - 1))
    stiff_prev = columns(coupling_of(prev[2], table, section > 0))
    rows[:, :matches] = jnp.where(even, own_rows, prev_rows)
    rows[:, matches:] = jnp.where(even, prev_rows, own_rows)
    for part in range(2):
        for chunk in range(chunks):
            entry[part, pl.ds(count + chunk, 1), :] = field[part, pl.ds(chunk * SUB, 1), :]
            entry[part, pl.ds(count + chunks + chunk, 1), :] = field[
                part, pl.ds(blocks - SUB * chunks + chunk * SUB + SUB - 1, 1), :
            ]
    send_edges(entry, halo_a, halo_b, count, chunks)
    listed.wait()

    def take(slot, row):
        for part in range(2):
            taken[part, pl.ds(slot, 1), :] = field[part, pl.ds(row, 1), :]

    each_slot(matches, lambda j: scalars[0, j], take)

    def place(values, coupling, at, send):
        stiff[at : at + matches, :] = coupling
        for part in range(2):
            value = values[part]
            entry[part, at : at + matches, :] = value
            send[part] = value * coupling

    @pl.when(even)
    def _():
        place(own_entry, stiff_own, 0, send_x)
        place(taken, stiff_prev, matches, send_z)

    @pl.when(jnp.logical_not(even))
    def _():
        place(taken, stiff_prev, 0, send_x)
        place(own_entry, stiff_own, matches, send_z)


def relate(rows_line, stiff, picked, column, same, weight, factor, chunks, blocks):
    count = rows_line.shape[1]
    total = count + 2 * chunks
    last = blocks - SUB * chunks + SUB - 1
    column[:count, :] = columns(rows_line[...].astype(jnp.float32))
    edge = lax.broadcasted_iota(jnp.int32, (chunks, LANES), 0) * SUB
    column[count : count + chunks, :] = edge.astype(jnp.float32)
    column[count + chunks :, :] = (edge + last).astype(jnp.float32)
    place = lax.broadcasted_iota(jnp.int32, (1, LANES), 1)
    edge_line = jnp.where(place < chunks, place * SUB, (place - chunks) * SUB + last)
    edge_line = jnp.where(place < 2 * chunks, edge_line, -1).astype(jnp.float32)

    def band(step, carry):
        at = pl.ds(pl.multiple_of(step * 32, 32), 32)
        col = column[at, :]
        for piece in range(count // LANES):
            cut = slice(piece * LANES, (piece + 1) * LANES)
            equal = col == rows_line[:, cut].astype(jnp.float32)
            same[at, cut] = equal.astype(jnp.float32).astype(jnp.bfloat16)
        same[at, count:] = (col == edge_line).astype(jnp.float32).astype(jnp.bfloat16)
        return carry

    lax.fori_loop(0, total // 32, band, 0)
    spring_here = picked[...]
    inverse = 1.0 / (4.0 * spring_here + summed(same[:, :count], stiff[...], 3))
    weight[...] = 4.0 * spring_here * inverse
    factor[...] = 0.8 * inverse


def stencil(field, nearby, start, chunks, top=False, bottom=False):
    span = SUB * chunks
    lane = lax.broadcasted_iota(jnp.int32, (SUB, LANES), 1)
    sub = lax.broadcasted_iota(jnp.int32, (SUB, LANES), 0)
    for part in range(2):

        def at(offset):
            return field[part, pl.ds(start + offset, SUB), :]

        before = jnp.zeros((SUB, LANES), jnp.float32)
        here = at(0)
        for chunk in range(chunks):
            offset = chunk * SUB
            after = at(offset + SUB) if chunk < chunks - 1 else jnp.zeros((SUB, LANES), jnp.float32)
            if top:
                up = jnp.where(sub == 0, 0.0, pltpu.roll(here, 1, 0))
            else:
                up = jnp.where(sub == 0, at(offset - span + SUB - 1), at(offset - 1))
            if bottom:
                down = jnp.where(sub == SUB - 1, 0.0, pltpu.roll(here, SUB - 1, 0))
            else:
                down = jnp.where(sub == SUB - 1, at(offset + span - SUB + 1), at(offset + 1))
            left = pltpu.roll(jnp.where(lane == LANES - 1, before, here), 1, 1)
            right = pltpu.roll(jnp.where(lane == 0, after, here), LANES - 1, 1)
            nearby[part, pl.ds(start + offset, SUB), :] = 0.2 * (((up + down) + (left + right)) + here)
            before, here = here, after


def strips_all(chunks, field, nearby):
    blocks = field.shape[1]
    span = SUB * chunks
    strips = blocks // span
    stencil(field, nearby, 0, chunks, top=True)
    stencil(field, nearby, blocks - span, chunks, bottom=True)
    group = math.gcd(strips - 2, GROUP)

    def some(step, carry):
        for inner in range(group):
            stencil(field, nearby, pl.multiple_of((1 + step * group + inner) * span, SUB), chunks)
        return carry

    lax.fori_loop(0, (strips - 2) // group, some, 0)


def each_entry(chunks, rows, blocks, take):
    count = rows.shape[1]
    each_slot(count, lambda j: rows[0, j], take)
    for chunk in range(chunks):
        take(count + chunk, chunk * SUB)
        take(count + chunks + chunk, blocks - SUB * chunks + chunk * SUB + SUB - 1)


def halo_rows(got_a, got_b):
    odd_tile = parity("tile") == 1
    return [
        (
            0.2 * jnp.where(odd_tile, got_a[part], got_b[part]),
            0.2 * jnp.where(odd_tile, got_b[part], got_a[part]),
        )
        for part in range(2)
    ]


def add_halo(field, halos, chunks):
    last = field.shape[1] - SUB * chunks + SUB - 1
    for part, (above, below) in enumerate(halos):
        for chunk in range(chunks):
            for start, halo in ((0, above), (last, below)):
                at = pl.ds(start + chunk * SUB, 1)
                field[part, at, :] = field[part, at, :] + halo[chunk : chunk + 1, :]


def start_kernel(chunks, rows, rows_line, stiff, spring, field, nearby, base, same, weight, factor, picked, column):
    strips_all(chunks, field, nearby)

    def take(slot, row):
        picked[pl.ds(slot, 1), :] = spring[pl.ds(row, 1), :]
        for part in range(2):
            base[part, pl.ds(slot, 1), :] = nearby[part, pl.ds(row, 1), :]

    each_entry(chunks, rows, field.shape[1], take)
    relate(rows_line, stiff, picked, column, same, weight, factor, chunks, field.shape[1])


def scatter_inner_kernel(chunks, rows, entry, stale, field, nearby, base):
    def put(slot, row):
        for part in range(2):
            field[part, pl.ds(row, 1), :] = entry[part, pl.ds(slot, 1), :]

    each_slot(rows.shape[1], lambda j: rows[0, j], put)
    strips_all(chunks, field, nearby)

    def take(slot, row):
        for part in range(2):
            base[part, pl.ds(slot, 1), :] = nearby[part, pl.ds(row, 1), :]

    each_entry(chunks, rows, field.shape[1], take)


def settle_kernel(chunks, got_a, got_b, entry, raw, same, weight, factor, stiff, stale, nearby, base):
    count = stiff.shape[0]
    halos = halo_rows(got_a, got_b)
    add_halo(nearby, halos, chunks)
    unused = same.shape[1] - count - 2 * chunks
    edges = jnp.concatenate(
        [
            jnp.concatenate([above, below, jnp.zeros((unused, LANES), jnp.float32)], axis=0)
            for above, below in halos
        ],
        axis=1,
    )
    outside = summed(same[:, count:], edges)
    for part in range(2):
        value = entry[part]
        base[part] = value + weight[...] * (
            (raw[part] - value) + outside[:, part * LANES : (part + 1) * LANES]
        )


def new_entries(got_x, got_z, old, base, same, factor, stiff):
    matches = got_x.shape[1]
    count = 2 * matches
    term = jnp.concatenate(
        [
            jnp.concatenate(
                [
                    got[part] - stiff[at : at + matches, :] * old[part, at : at + matches, :]
                    for at, got in ((0, got_x), (matches, got_z))
                ],
                axis=0,
            )
            for part in range(2)
        ],
        axis=1,
    )
    total = summed(same[:, :count], term)
    return [base[part] + factor[...] * total[:, part * LANES : (part + 1) * LANES] for part in range(2)]


def step_kernel(chunks, got_x, got_z, old, base, same, factor, stiff, entry, send_x, send_z, halo_a, halo_b):
    matches = got_x.shape[1]
    count = 2 * matches
    for part, value in enumerate(new_entries(got_x, got_z, old, base, same, factor, stiff)):
        entry[part] = value
        send_x[part] = value[:matches] * stiff[:matches, :]
        send_z[part] = value[matches:count] * stiff[matches:, :]
    send_edges(entry, halo_a, halo_b, count, chunks)


def last_kernel(rows, stale, got_x, got_z, old, base, same, factor, stiff, nearby, out, entry, sem):
    for part, value in enumerate(new_entries(got_x, got_z, old, base, same, factor, stiff)):
        entry[part] = value
    stores = load_parts(nearby, out, sem, LOADS)
    for part in range(2):

        def put(slot, row):
            nearby[part, pl.ds(row, 1), :] = entry[part, pl.ds(slot, 1), :]

        each_slot(rows.shape[1], lambda j: rows[0, j], put)
        for copy in stores[part * LOADS : (part + 1) * LOADS]:
            copy.start()
    for copy in stores:
        copy.wait()


def exchange(array, axis, pairs):
    return lax.ppermute(array, axis, pairs)


def pairs_from(first, size):
    out = []
    for i in range(first, size - 1, 2):
        out += [(i, i + 1), (i + 1, i)]
    return out


def on_device(displacement, spring, stiff_table, match_blocks, match_class):
    fields, single, height, breadth = displacement.shape
    chunks = breadth // LANES
    blocks = height * chunks
    matches = match_blocks.shape[2]
    count = 2 * matches
    total = count + 2 * chunks
    sections, tiles = lax.axis_size("sec"), lax.axis_size("tile")
    near, far = pairs_from(0, sections), pairs_from(1, sections)
    near_tile, far_tile = pairs_from(0, tiles), pairs_from(1, tiles)

    def tiled(x):
        lead = x.shape[:-2]
        x = x.reshape(lead + (height // SUB, SUB, chunks, LANES))
        return jnp.swapaxes(x, -3, -2).reshape(lead + (blocks, LANES))

    def untiled(x):
        lead = x.shape[:-2]
        x = x.reshape(lead + (height // SUB, chunks, SUB, LANES))
        return jnp.swapaxes(x, -3, -2).reshape(lead + (height, breadth))

    def call(name, kernel, ins, outs, vmem=24 << 20, **more):
        return pl.pallas_call(
            kernel,
            in_specs=ins,
            out_specs=tuple(spec for spec, _ in outs),
            out_shape=tuple(shape for _, shape in outs),
            compiler_params=pltpu.CompilerParams(vmem_limit_bytes=vmem),
            name=name,
            **more,
        )

    halo = (VM, f32(fields, chunks, LANES))
    send = (VM, f32(fields, matches, LANES))
    entries = (VM, f32(fields, total, LANES))
    big = (VM, f32(fields, blocks, LANES))
    wide = (VM, f32(total, LANES))
    rows_shape = (VM, jax.ShapeDtypeStruct((1, count), jnp.int32))

    packed = jnp.concatenate([match_blocks, match_class[:, None]], axis=0)
    prev = exchange(packed, "sec", [(i, i + 1) for i in range(sections - 1)])
    staging = [
        pltpu.VMEM((1, matches), jnp.int32),
        pltpu.SMEM((1, matches), jnp.int32),
    ]
    field, own_entry = call(
        "own",
        functools.partial(own_kernel, chunks),
        [VM, HBM],
        [big, send],
        scratch_shapes=staging + [pltpu.SemaphoreType.DMA, pltpu.SemaphoreType.DMA((2 * LOADS,))],
        vmem=OWN_VMEM << 20,
    )(packed, tiled(displacement[:, 0]))
    entry, stiff, rows, send_x, send_z, halo_a, halo_b = call(
        "first",
        functools.partial(first_kernel, chunks),
        [VM] * 5,
        [entries, (VM, f32(count, LANES)), rows_shape, send, send, halo, halo],
        scratch_shapes=staging
        + [pltpu.VMEM((fields, matches, LANES), jnp.float32), pltpu.SemaphoreType.DMA],
    )(stiff_table[None], packed, prev, field, own_entry)

    for sweep in range(ITERS):
        got_x = exchange(send_x, "sec", near)
        got_z = exchange(send_z, "sec", far)
        got_a = exchange(halo_a, "tile", near_tile)
        got_b = exchange(halo_b, "tile", far_tile)
        if sweep == 0:
            nearby, base, same, weight, factor = call(
                "start",
                functools.partial(start_kernel, chunks),
                [SM, VM, VM, VM, VM],
                [big, entries, (VM, jax.ShapeDtypeStruct((total, count + LANES), jnp.bfloat16)), wide, wide],
                scratch_shapes=[pltpu.VMEM((total, LANES), jnp.float32)] * 2,
            )(rows, rows, stiff, tiled(spring[0]), field)
        else:
            field, nearby, base = call(
                "inner",
                functools.partial(scatter_inner_kernel, chunks),
                [SM] + [VM] * 2,
                [big, big, entries],
                input_output_aliases={2: 0},
            )(rows, entry, nearby)
        nearby, base = call(
            "settle",
            functools.partial(settle_kernel, chunks),
            [VM] * 9,
            [big, entries],
            input_output_aliases={8: 0},
        )(got_a, got_b, entry, base, same, weight, factor, stiff, nearby)
        if sweep < ITERS - 1:
            entry, send_x, send_z, halo_a, halo_b = call(
                "step", functools.partial(step_kernel, chunks), [VM] * 7, [entries, send, send, halo, halo]
            )(got_x, got_z, entry, base, same, factor, stiff)
    _, out = call(
        "last",
        last_kernel,
        [SM] + [VM] * 8,
        [big, (HBM, f32(fields, blocks, LANES))],
        scratch_shapes=[
            pltpu.VMEM((fields, total, LANES), jnp.float32),
            pltpu.SemaphoreType.DMA((2 * LOADS,)),
        ],
        input_output_aliases={1: 0},
    )(rows, nearby, got_x, got_z, entry, base, same, factor, stiff)
    return untiled(out)[:, None]


def solution(mesh):
    placed = (
        P(None, "sec", "tile", None),
        P("sec", "tile", None),
        P(),
        P(None, "sec", "tile"),
        P("sec", "tile"),
    )
    return jax.shard_map(
        on_device,
        mesh=mesh,
        in_specs=placed,
        out_specs=P(None, "sec", "tile", None),
        check_vma=False,
    )
```

```python
import functools
import math
import jax
import jax.numpy as jnp
from jax import lax
from jax.experimental import pallas as pl
from jax.experimental.pallas import tpu as pltpu
from jax.sharding import PartitionSpec as P

ITERS = 3
LOADS = 4
GROUP = 6
OWN_VMEM = 47
LANES = 128
SUB = 8

VM = pl.BlockSpec(memory_space=pltpu.VMEM)
SM = pl.BlockSpec(memory_space=pltpu.SMEM)
HBM = pl.BlockSpec(memory_space=pltpu.MemorySpace.HBM)


def f32(*shape):
    return jax.ShapeDtypeStruct(shape, jnp.float32)


def tile_row(block, chunks):
    bits, low = chunks.bit_length() - 1, SUB.bit_length() - 1
    row = block >> bits
    return ((row >> low) << (bits + low)) | ((block & (chunks - 1)) << low) | (row & (SUB - 1))


def pieces(x, count):
    out = []
    for _ in range(count):
        out.append(x.astype(jnp.bfloat16))
        x = x - out[-1].astype(jnp.float32)
    return out


def summed(same, x, count=2):
    out = None
    for piece in pieces(x, count):
        product = jnp.dot(same, piece, preferred_element_type=jnp.float32)
        out = product if out is None else out + product
    return out


def parity(axis):
    return lax.axis_index(axis) % 2


def columns(line):
    return jnp.concatenate(
        [
            jnp.broadcast_to(line[:, at : at + LANES], (LANES, LANES)).T
            for at in range(0, line.shape[1], LANES)
        ],
        axis=0,
    )


def each_slot(count, rows, body):
    def some(step, carry):
        for inner in range(16):
            slot = step * 16 + inner
            body(slot, rows(slot))
        return carry

    lax.fori_loop(0, count // 16, some, 0)


def into_smem(line, staged, scalars, sem):
    staged[...] = line
    copy = pltpu.make_async_copy(staged, scalars, sem)
    copy.start()
    return copy


def load_parts(source, target, sem, pieces_each):
    rows = source.shape[1] // pieces_each
    copies = []
    for part in range(source.shape[0]):
        for piece in range(pieces_each):
            at = pl.ds(piece * rows, rows)
            copies.append(
                pltpu.make_async_copy(
                    source.at[part, at, :], target.at[part, at, :], sem.at[part * pieces_each + piece]
                )
            )
    return copies


def coupling_of(classes, table, alive):
    out = jnp.zeros(classes.shape, jnp.float32)
    for level in range(table.shape[1]):
        out = jnp.where(classes == level, table[:, level : level + 1], out)
    return out * alive.astype(jnp.float32)


def own_kernel(chunks, packed, displacement, field, entry, staged, scalars, sem, load_sem):
    loads = load_parts(displacement, field, load_sem, LOADS)
    for copy in loads:
        copy.start()
    listed = into_smem(tile_row(packed[0], chunks), staged, scalars, sem)
    listed.wait()
    for part in range(2):
        for copy in loads[part * LOADS : (part + 1) * LOADS]:
            copy.wait()

        def take(slot, row):
            entry[part, pl.ds(slot, 1), :] = field[part, pl.ds(row, 1), :]

        each_slot(packed.shape[2], lambda j: scalars[0, j], take)


def first_kernel(chunks, table, packed, prev, field, own_entry, entry, stiff, rows, send_x, send_z, edges, staged, scalars, taken, sem):
    blocks = field.shape[1]
    matches = own_entry.shape[1]
    count = 2 * matches
    own_rows, prev_rows = tile_row(packed[0], chunks), tile_row(prev[1], chunks)
    listed = into_smem(prev_rows, staged, scalars, sem)
    even = parity("sec") == 0
    section = lax.axis_index("sec")
    stiff_own = columns(coupling_of(packed[2], table, section < lax.axis_size("sec") - 1))
    stiff_prev = columns(coupling_of(prev[2], table, section > 0))
    rows[:, :matches] = jnp.where(even, own_rows, prev_rows)
    rows[:, matches:] = jnp.where(even, prev_rows, own_rows)
    for part in range(2):
        for chunk in range(chunks):
            entry[part, pl.ds(count + chunk, 1), :] = field[part, pl.ds(chunk * SUB, 1), :]
            entry[part, pl.ds(count + chunks + chunk, 1), :] = field[
                part, pl.ds(blocks - SUB * chunks + chunk * SUB + SUB - 1, 1), :
            ]
    edges[...] = entry[:, count:, :]
    listed.wait()

    def take(slot, row):
        for part in range(2):
            taken[part, pl.ds(slot, 1), :] = field[part, pl.ds(row, 1), :]

    each_slot(matches, lambda j: scalars[0, j], take)

    def place(values, coupling, at, send):
        stiff[at : at + matches, :] = coupling
        for part in range(2):
            value = values[part]
            entry[part, at : at + matches, :] = value
            send[part] = value * coupling

    @pl.when(even)
    def _():
        place(own_entry, stiff_own, 0, send_x)
        place(taken, stiff_prev, matches, send_z)

    @pl.when(jnp.logical_not(even))
    def _():
        place(taken, stiff_prev, 0, send_x)
        place(own_entry, stiff_own, matches, send_z)


def relate(rows_line, stiff, picked, column, same, weight, factor, chunks, blocks):
    count = rows_line.shape[1]
    total = count + 2 * chunks
    last = blocks - SUB * chunks + SUB - 1
    column[:count, :] = columns(rows_line[...].astype(jnp.float32))
    edge = lax.broadcasted_iota(jnp.int32, (chunks, LANES), 0) * SUB
    column[count : count + chunks, :] = edge.astype(jnp.float32)
    column[count + chunks :, :] = (edge + last).astype(jnp.float32)
    place = lax.broadcasted_iota(jnp.int32, (1, LANES), 1)
    edge_line = jnp.where(place < chunks, place * SUB, (place - chunks) * SUB + last)
    edge_line = jnp.where(place < 2 * chunks, edge_line, -1).astype(jnp.float32)

    def band(step, carry):
        at = pl.ds(pl.multiple_of(step * 32, 32), 32)
        col = column[at, :]
        for piece in range(count // LANES):
            cut = slice(piece * LANES, (piece + 1) * LANES)
            equal = col == rows_line[:, cut].astype(jnp.float32)
            same[at, cut] = equal.astype(jnp.float32).astype(jnp.bfloat16)
        same[at, count:] = (col == edge_line).astype(jnp.float32).astype(jnp.bfloat16)
        return carry

    lax.fori_loop(0, total // 32, band, 0)
    spring_here = picked[...]
    inverse = 1.0 / (4.0 * spring_here + summed(same[:, :count], stiff[...], 3))
    weight[...] = 4.0 * spring_here * inverse
    factor[...] = 0.8 * inverse


def stencil(field, nearby, start, chunks, top=False, bottom=False):
    span = SUB * chunks
    lane = lax.broadcasted_iota(jnp.int32, (SUB, LANES), 1)
    sub = lax.broadcasted_iota(jnp.int32, (SUB, LANES), 0)
    for part in range(2):

        def at(offset):
            return field[part, pl.ds(start + offset, SUB), :]

        before = jnp.zeros((SUB, LANES), jnp.float32)
        here = at(0)
        for chunk in range(chunks):
            offset = chunk * SUB
            after = at(offset + SUB) if chunk < chunks - 1 else jnp.zeros((SUB, LANES), jnp.float32)
            if top:
                up = jnp.where(sub == 0, 0.0, pltpu.roll(here, 1, 0))
            else:
                up = jnp.where(sub == 0, at(offset - span + SUB - 1), at(offset - 1))
            if bottom:
                down = jnp.where(sub == SUB - 1, 0.0, pltpu.roll(here, SUB - 1, 0))
            else:
                down = jnp.where(sub == SUB - 1, at(offset + span - SUB + 1), at(offset + 1))
            left = pltpu.roll(jnp.where(lane == LANES - 1, before, here), 1, 1)
            right = pltpu.roll(jnp.where(lane == 0, after, here), LANES - 1, 1)
            nearby[part, pl.ds(start + offset, SUB), :] = 0.2 * (((up + down) + (left + right)) + here)
            before, here = here, after


def strips_all(chunks, field, nearby):
    blocks = field.shape[1]
    span = SUB * chunks
    strips = blocks // span
    stencil(field, nearby, 0, chunks, top=True)
    stencil(field, nearby, blocks - span, chunks, bottom=True)
    group = math.gcd(strips - 2, GROUP)

    def some(step, carry):
        for inner in range(group):
            stencil(field, nearby, pl.multiple_of((1 + step * group + inner) * span, SUB), chunks)
        return carry

    lax.fori_loop(0, (strips - 2) // group, some, 0)


def each_entry(chunks, rows, blocks, take):
    count = rows.shape[1]
    each_slot(count, lambda j: rows[0, j], take)
    for chunk in range(chunks):
        take(count + chunk, chunk * SUB)
        take(count + chunks + chunk, blocks - SUB * chunks + chunk * SUB + SUB - 1)


def halo_rows(got_a, got_b):
    tile, tiles = lax.axis_index("tile"), lax.axis_size("tile")
    chunks = got_a.shape[1] // 2
    odd = tile % 2 == 1
    has_above, has_below = tile > 0, tile < tiles - 1
    out = []
    for part in range(2):
        (a_top, a_bottom), (b_top, b_bottom) = (
            (got[part, :chunks, :], got[part, chunks:, :]) for got in (got_a, got_b)
        )
        above, below = jnp.where(odd, a_bottom, b_bottom), jnp.where(odd, b_top, a_top)
        out.append((jnp.where(has_above, 0.2 * above, 0.0), jnp.where(has_below, 0.2 * below, 0.0)))
    return out


def add_halo(field, halos, chunks):
    last = field.shape[1] - SUB * chunks + SUB - 1
    for part, (above, below) in enumerate(halos):
        for chunk in range(chunks):
            for start, halo in ((0, above), (last, below)):
                at = pl.ds(start + chunk * SUB, 1)
                field[part, at, :] = field[part, at, :] + halo[chunk : chunk + 1, :]


def start_kernel(chunks, rows, rows_line, stiff, spring, field, nearby, base, same, weight, factor, picked, column):
    strips_all(chunks, field, nearby)

    def take(slot, row):
        picked[pl.ds(slot, 1), :] = spring[pl.ds(row, 1), :]
        for part in range(2):
            base[part, pl.ds(slot, 1), :] = nearby[part, pl.ds(row, 1), :]

    each_entry(chunks, rows, field.shape[1], take)
    relate(rows_line, stiff, picked, column, same, weight, factor, chunks, field.shape[1])


def scatter_inner_kernel(chunks, rows, entry, stale, field, nearby, base):
    def put(slot, row):
        for part in range(2):
            field[part, pl.ds(row, 1), :] = entry[part, pl.ds(slot, 1), :]

    each_slot(rows.shape[1], lambda j: rows[0, j], put)
    strips_all(chunks, field, nearby)

    def take(slot, row):
        for part in range(2):
            base[part, pl.ds(slot, 1), :] = nearby[part, pl.ds(row, 1), :]

    each_entry(chunks, rows, field.shape[1], take)


def settle_kernel(chunks, got_a, got_b, entry, raw, same, weight, factor, stiff, stale, nearby, base):
    count = stiff.shape[0]
    halos = halo_rows(got_a, got_b)
    add_halo(nearby, halos, chunks)
    unused = same.shape[1] - count - 2 * chunks
    edges = jnp.concatenate(
        [
            jnp.concatenate([above, below, jnp.zeros((unused, LANES), jnp.float32)], axis=0)
            for above, below in halos
        ],
        axis=1,
    )
    outside = summed(same[:, count:], edges)
    for part in range(2):
        value = entry[part]
        base[part] = value + weight[...] * (
            (raw[part] - value) + outside[:, part * LANES : (part + 1) * LANES]
        )


def new_entries(got_x, got_z, old, base, same, factor, stiff):
    matches = got_x.shape[1]
    count = 2 * matches
    term = jnp.concatenate(
        [
            jnp.concatenate(
                [
                    got[part] - stiff[at : at + matches, :] * old[part, at : at + matches, :]
                    for at, got in ((0, got_x), (matches, got_z))
                ],
                axis=0,
            )
            for part in range(2)
        ],
        axis=1,
    )
    total = summed(same[:, :count], term)
    return [base[part] + factor[...] * total[:, part * LANES : (part + 1) * LANES] for part in range(2)]


def step_kernel(got_x, got_z, old, base, same, factor, stiff, entry, send_x, send_z, edges):
    matches = got_x.shape[1]
    count = 2 * matches
    for part, value in enumerate(new_entries(got_x, got_z, old, base, same, factor, stiff)):
        entry[part] = value
        send_x[part] = value[:matches] * stiff[:matches, :]
        send_z[part] = value[matches:count] * stiff[matches:, :]
    edges[...] = entry[:, count:, :]


def last_kernel(rows, stale, got_x, got_z, old, base, same, factor, stiff, nearby, out, entry, sem):
    for part, value in enumerate(new_entries(got_x, got_z, old, base, same, factor, stiff)):
        entry[part] = value
    stores = load_parts(nearby, out, sem, LOADS)
    for part in range(2):

        def put(slot, row):
            nearby[part, pl.ds(row, 1), :] = entry[part, pl.ds(slot, 1), :]

        each_slot(rows.shape[1], lambda j: rows[0, j], put)
        for copy in stores[part * LOADS : (part + 1) * LOADS]:
            copy.start()
    for copy in stores:
        copy.wait()


def exchange(array, axis, pairs):
    return lax.ppermute(array, axis, pairs)


def pairs_from(first, size):
    out = []
    for i in range(first, size - 1, 2):
        out += [(i, i + 1), (i + 1, i)]
    return out


def on_device(displacement, spring, stiff_table, match_blocks, match_class):
    fields, _, height, breadth = displacement.shape
    chunks = breadth // LANES
    blocks = height * chunks
    matches = match_blocks.shape[2]
    count = 2 * matches
    total = count + 2 * chunks
    sections, tiles = lax.axis_size("sec"), lax.axis_size("tile")
    near, far = pairs_from(0, sections), pairs_from(1, sections)
    near_tile = pairs_from(0, tiles)
    relay = [(i - 1, i + 1) for i in range(1, tiles - 1, 2)] + [(i + 2, i) for i in range(1, tiles - 1, 2)]
    senders, takers = {a for a, _ in relay}, {b for _, b in relay}
    relay += [(b, a) for a, b in relay if b not in senders and a not in takers]

    def tiled(x):
        lead = x.shape[:-2]
        x = x.reshape(lead + (height // SUB, SUB, chunks, LANES))
        return jnp.swapaxes(x, -3, -2).reshape(lead + (blocks, LANES))

    def untiled(x):
        lead = x.shape[:-2]
        x = x.reshape(lead + (height // SUB, chunks, SUB, LANES))
        return jnp.swapaxes(x, -3, -2).reshape(lead + (height, breadth))

    def call(kernel, ins, outs, vmem=24 << 20, **more):
        return pl.pallas_call(
            kernel,
            in_specs=ins,
            out_specs=tuple(spec for spec, _ in outs),
            out_shape=tuple(shape for _, shape in outs),
            compiler_params=pltpu.CompilerParams(vmem_limit_bytes=vmem),
            **more,
        )

    halo = (VM, f32(fields, 2 * chunks, LANES))
    send = (VM, f32(fields, matches, LANES))
    entries = (VM, f32(fields, total, LANES))
    big = (VM, f32(fields, blocks, LANES))
    wide = (VM, f32(total, LANES))
    rows_shape = (VM, jax.ShapeDtypeStruct((1, count), jnp.int32))

    packed = jnp.concatenate([match_blocks, match_class[:, None]], axis=0)
    prev = exchange(packed, "sec", [(i, i + 1) for i in range(sections - 1)])
    staging = [
        pltpu.VMEM((1, matches), jnp.int32),
        pltpu.SMEM((1, matches), jnp.int32),
    ]
    field, own_entry = call(
        functools.partial(own_kernel, chunks),
        [VM, HBM],
        [big, send],
        scratch_shapes=staging + [pltpu.SemaphoreType.DMA, pltpu.SemaphoreType.DMA((2 * LOADS,))],
        vmem=OWN_VMEM << 20,
    )(packed, tiled(displacement[:, 0]))
    entry, stiff, rows, send_x, send_z, edges = call(
        functools.partial(first_kernel, chunks),
        [VM] * 5,
        [entries, (VM, f32(count, LANES)), rows_shape, send, send, halo],
        scratch_shapes=staging
        + [pltpu.VMEM((fields, matches, LANES), jnp.float32), pltpu.SemaphoreType.DMA],
    )(stiff_table[None], packed, prev, field, own_entry)

    for sweep in range(ITERS):
        got_x = exchange(send_x, "sec", near)
        got_z = exchange(send_z, "sec", far)
        got_a = exchange(edges, "tile", near_tile)
        got_b = exchange(got_a, "tile", relay)
        if sweep == 0:
            nearby, base, same, weight, factor = call(
                functools.partial(start_kernel, chunks),
                [SM, VM, VM, VM, VM],
                [big, entries, (VM, jax.ShapeDtypeStruct((total, count + LANES), jnp.bfloat16)), wide, wide],
                scratch_shapes=[pltpu.VMEM((total, LANES), jnp.float32)] * 2,
            )(rows, rows, stiff, tiled(spring[0]), field)
        else:
            field, nearby, base = call(
                functools.partial(scatter_inner_kernel, chunks),
                [SM] + [VM] * 2,
                [big, big, entries],
                input_output_aliases={2: 0},
            )(rows, entry, nearby)
        nearby, base = call(
            functools.partial(settle_kernel, chunks), [VM] * 9, [big, entries], input_output_aliases={8: 0}
        )(got_a, got_b, entry, base, same, weight, factor, stiff, nearby)
        if sweep < ITERS - 1:
            entry, send_x, send_z, edges = call(
                step_kernel, [VM] * 7, [entries, send, send, halo]
            )(got_x, got_z, entry, base, same, factor, stiff)
    _, out = call(
        last_kernel,
        [SM] + [VM] * 8,
        [big, (HBM, f32(fields, blocks, LANES))],
        scratch_shapes=[
            pltpu.VMEM((fields, total, LANES), jnp.float32),
            pltpu.SemaphoreType.DMA((2 * LOADS,)),
        ],
        input_output_aliases={1: 0},
    )(rows, nearby, got_x, got_z, entry, base, same, factor, stiff)
    return untiled(out)[:, None]


def solution(mesh):
    placed = (
        P(None, "sec", "tile", None),
        P("sec", "tile", None),
        P(),
        P(None, "sec", "tile"),
        P("sec", "tile"),
    )
    return jax.shard_map(
        on_device,
        mesh=mesh,
        in_specs=placed,
        out_specs=P(None, "sec", "tile", None),
        check_vma=False,
    )
```

```python
import functools
import math
import jax
import jax.numpy as jnp
from jax import lax
from jax.experimental import pallas as pl
from jax.experimental.pallas import tpu as pltpu
from jax.sharding import PartitionSpec as P

ITERS = 3
LOADS = 1
GROUP = 15
OWN_VMEM = 47
LANES = 128
SUB = 8

VM = pl.BlockSpec(memory_space=pltpu.VMEM)
SM = pl.BlockSpec(memory_space=pltpu.SMEM)
HBM = pl.BlockSpec(memory_space=pltpu.MemorySpace.HBM)


def f32(*shape):
    return jax.ShapeDtypeStruct(shape, jnp.float32)


def tile_row(block, chunks):
    bits, low = chunks.bit_length() - 1, SUB.bit_length() - 1
    row = block >> bits
    return ((row >> low) << (bits + low)) | ((block & (chunks - 1)) << low) | (row & (SUB - 1))


def pieces(x, count):
    out = []
    for _ in range(count):
        out.append(x.astype(jnp.bfloat16))
        x = x - out[-1].astype(jnp.float32)
    return out


def summed(same, x, count=2):
    out = None
    for piece in pieces(x, count):
        product = jnp.dot(same, piece, preferred_element_type=jnp.float32)
        out = product if out is None else out + product
    return out


def parity(axis):
    return lax.axis_index(axis) % 2


def columns(line):
    return jnp.concatenate(
        [
            jnp.broadcast_to(line[:, at : at + LANES], (LANES, LANES)).T
            for at in range(0, line.shape[1], LANES)
        ],
        axis=0,
    )


def each_slot(count, rows, body):
    def some(step, carry):
        for inner in range(16):
            slot = step * 16 + inner
            body(slot, rows(slot))
        return carry

    lax.fori_loop(0, count // 16, some, 0)


def into_smem(line, staged, scalars, sem):
    staged[...] = line
    copy = pltpu.make_async_copy(staged, scalars, sem)
    copy.start()
    return copy


def load_parts(source, target, sem, pieces_each):
    rows = source.shape[1] // pieces_each
    copies = []
    for part in range(source.shape[0]):
        for piece in range(pieces_each):
            at = pl.ds(piece * rows, rows)
            copies.append(
                pltpu.make_async_copy(
                    source.at[part, at, :], target.at[part, at, :], sem.at[part * pieces_each + piece]
                )
            )
    return copies


def coupling_of(classes, table, alive):
    out = jnp.zeros(classes.shape, jnp.float32)
    for level in range(table.shape[1]):
        out = jnp.where(classes == level, table[:, level : level + 1], out)
    return out * alive.astype(jnp.float32)


def own_kernel(chunks, packed, displacement, field, entry, staged, scalars, sem, load_sem):
    loads = load_parts(displacement, field, load_sem, LOADS)
    for copy in loads:
        copy.start()
    listed = into_smem(tile_row(packed[0], chunks), staged, scalars, sem)
    listed.wait()
    for part in range(2):
        for copy in loads[part * LOADS : (part + 1) * LOADS]:
            copy.wait()

        def take(slot, row):
            entry[part, pl.ds(slot, 1), :] = field[part, pl.ds(row, 1), :]

        each_slot(packed.shape[2], lambda j: scalars[0, j], take)


def first_kernel(chunks, table, packed, prev, field, own_entry, entry, stiff, rows, send_x, send_z, edges, staged, scalars, taken, sem):
    blocks = field.shape[1]
    matches = own_entry.shape[1]
    count = 2 * matches
    own_rows, prev_rows = tile_row(packed[0], chunks), tile_row(prev[1], chunks)
    listed = into_smem(prev_rows, staged, scalars, sem)
    even = parity("sec") == 0
    section = lax.axis_index("sec")
    stiff_own = columns(coupling_of(packed[2], table, section < lax.axis_size("sec") - 1))
    stiff_prev = columns(coupling_of(prev[2], table, section > 0))
    rows[:, :matches] = jnp.where(even, own_rows, prev_rows)
    rows[:, matches:] = jnp.where(even, prev_rows, own_rows)
    for part in range(2):
        for chunk in range(chunks):
            entry[part, pl.ds(count + chunk, 1), :] = field[part, pl.ds(chunk * SUB, 1), :]
            entry[part, pl.ds(count + chunks + chunk, 1), :] = field[
                part, pl.ds(blocks - SUB * chunks + chunk * SUB + SUB - 1, 1), :
            ]
    edges[...] = entry[:, count:, :]
    listed.wait()

    def take(slot, row):
        for part in range(2):
            taken[part, pl.ds(slot, 1), :] = field[part, pl.ds(row, 1), :]

    each_slot(matches, lambda j: scalars[0, j], take)

    def place(values, coupling, at, send):
        stiff[at : at + matches, :] = coupling
        for part in range(2):
            value = values[part]
            entry[part, at : at + matches, :] = value
            send[part] = value * coupling

    @pl.when(even)
    def _():
        place(own_entry, stiff_own, 0, send_x)
        place(taken, stiff_prev, matches, send_z)

    @pl.when(jnp.logical_not(even))
    def _():
        place(taken, stiff_prev, 0, send_x)
        place(own_entry, stiff_own, matches, send_z)


def relate(rows_line, stiff, picked, column, same, weight, factor, chunks, blocks):
    count = rows_line.shape[1]
    total = count + 2 * chunks
    last = blocks - SUB * chunks + SUB - 1
    column[:count, :] = columns(rows_line[...].astype(jnp.float32))
    edge = lax.broadcasted_iota(jnp.int32, (chunks, LANES), 0) * SUB
    column[count : count + chunks, :] = edge.astype(jnp.float32)
    column[count + chunks :, :] = (edge + last).astype(jnp.float32)
    place = lax.broadcasted_iota(jnp.int32, (1, LANES), 1)
    edge_line = jnp.where(place < chunks, place * SUB, (place - chunks) * SUB + last)
    edge_line = jnp.where(place < 2 * chunks, edge_line, -1).astype(jnp.float32)

    def band(step, carry):
        at = pl.ds(pl.multiple_of(step * 32, 32), 32)
        col = column[at, :]
        for piece in range(count // LANES):
            cut = slice(piece * LANES, (piece + 1) * LANES)
            equal = col == rows_line[:, cut].astype(jnp.float32)
            same[at, cut] = equal.astype(jnp.float32).astype(jnp.bfloat16)
        same[at, count:] = (col == edge_line).astype(jnp.float32).astype(jnp.bfloat16)
        return carry

    lax.fori_loop(0, total // 32, band, 0)
    spring_here = picked[...]
    inverse = 1.0 / (4.0 * spring_here + summed(same[:, :count], stiff[...], 3))
    weight[...] = 4.0 * spring_here * inverse
    factor[...] = 0.8 * inverse


def stencil(field, nearby, start, chunks, top=False, bottom=False):
    span = SUB * chunks
    lane = lax.broadcasted_iota(jnp.int32, (SUB, LANES), 1)
    sub = lax.broadcasted_iota(jnp.int32, (SUB, LANES), 0)
    for part in range(2):

        def at(offset):
            return field[part, pl.ds(start + offset, SUB), :]

        before = jnp.zeros((SUB, LANES), jnp.float32)
        here = at(0)
        for chunk in range(chunks):
            offset = chunk * SUB
            after = at(offset + SUB) if chunk < chunks - 1 else jnp.zeros((SUB, LANES), jnp.float32)
            if top:
                up = jnp.where(sub == 0, 0.0, pltpu.roll(here, 1, 0))
            else:
                up = jnp.where(sub == 0, at(offset - span + SUB - 1), at(offset - 1))
            if bottom:
                down = jnp.where(sub == SUB - 1, 0.0, pltpu.roll(here, SUB - 1, 0))
            else:
                down = jnp.where(sub == SUB - 1, at(offset + span - SUB + 1), at(offset + 1))
            left = pltpu.roll(jnp.where(lane == LANES - 1, before, here), 1, 1)
            right = pltpu.roll(jnp.where(lane == 0, after, here), LANES - 1, 1)
            nearby[part, pl.ds(start + offset, SUB), :] = 0.2 * (((up + down) + (left + right)) + here)
            before, here = here, after


def strips_all(chunks, field, nearby):
    blocks = field.shape[1]
    span = SUB * chunks
    strips = blocks // span
    stencil(field, nearby, 0, chunks, top=True)
    stencil(field, nearby, blocks - span, chunks, bottom=True)
    group = math.gcd(strips - 2, GROUP)

    def some(step, carry):
        for inner in range(group):
            stencil(field, nearby, pl.multiple_of((1 + step * group + inner) * span, SUB), chunks)
        return carry

    lax.fori_loop(0, (strips - 2) // group, some, 0)


def each_entry(chunks, rows, blocks, take):
    count = rows.shape[1]
    each_slot(count, lambda j: rows[0, j], take)
    for chunk in range(chunks):
        take(count + chunk, chunk * SUB)
        take(count + chunks + chunk, blocks - SUB * chunks + chunk * SUB + SUB - 1)


def halo_rows(got_a, got_b):
    tile, tiles = lax.axis_index("tile"), lax.axis_size("tile")
    chunks = got_a.shape[1] // 2
    odd = tile % 2 == 1
    has_above, has_below = tile > 0, tile < tiles - 1
    out = []
    for part in range(2):
        (a_top, a_bottom), (b_top, b_bottom) = (
            (got[part, :chunks, :], got[part, chunks:, :]) for got in (got_a, got_b)
        )
        above, below = jnp.where(odd, a_bottom, b_bottom), jnp.where(odd, b_top, a_top)
        out.append((jnp.where(has_above, 0.2 * above, 0.0), jnp.where(has_below, 0.2 * below, 0.0)))
    return out


def add_halo(field, halos, chunks):
    last = field.shape[1] - SUB * chunks + SUB - 1
    for part, (above, below) in enumerate(halos):
        for chunk in range(chunks):
            for start, halo in ((0, above), (last, below)):
                at = pl.ds(start + chunk * SUB, 1)
                field[part, at, :] = field[part, at, :] + halo[chunk : chunk + 1, :]


def start_kernel(chunks, rows, rows_line, stiff, spring, field, nearby, base, same, weight, factor, picked, column):
    strips_all(chunks, field, nearby)

    def take(slot, row):
        picked[pl.ds(slot, 1), :] = spring[pl.ds(row, 1), :]
        for part in range(2):
            base[part, pl.ds(slot, 1), :] = nearby[part, pl.ds(row, 1), :]

    each_entry(chunks, rows, field.shape[1], take)
    relate(rows_line, stiff, picked, column, same, weight, factor, chunks, field.shape[1])


def scatter_inner_kernel(chunks, rows, entry, stale, field, nearby, base):
    def put(slot, row):
        for part in range(2):
            field[part, pl.ds(row, 1), :] = entry[part, pl.ds(slot, 1), :]

    each_slot(rows.shape[1], lambda j: rows[0, j], put)
    strips_all(chunks, field, nearby)

    def take(slot, row):
        for part in range(2):
            base[part, pl.ds(slot, 1), :] = nearby[part, pl.ds(row, 1), :]

    each_entry(chunks, rows, field.shape[1], take)


def settle_kernel(chunks, got_a, got_b, entry, raw, same, weight, factor, stiff, stale, nearby, base):
    count = stiff.shape[0]
    halos = halo_rows(got_a, got_b)
    add_halo(nearby, halos, chunks)
    unused = same.shape[1] - count - 2 * chunks
    edges = jnp.concatenate(
        [
            jnp.concatenate([above, below, jnp.zeros((unused, LANES), jnp.float32)], axis=0)
            for above, below in halos
        ],
        axis=1,
    )
    outside = summed(same[:, count:], edges)
    own = jnp.concatenate([entry[part, :count, :] * stiff[...] for part in range(2)], axis=1)
    total = summed(same[:, :count], own)
    for part in range(2):
        cut = slice(part * LANES, (part + 1) * LANES)
        value = entry[part]
        base[part] = (
            value
            + weight[...] * ((raw[part] - value) + outside[:, cut])
            - factor[...] * total[:, cut]
        )


def new_entries(got_x, got_z, base, same, factor):
    count = 2 * got_x.shape[1]
    got = jnp.concatenate(
        [jnp.concatenate([got_x[part], got_z[part]], axis=0) for part in range(2)], axis=1
    )
    total = summed(same[:, :count], got)
    return [base[part] + factor[...] * total[:, part * LANES : (part + 1) * LANES] for part in range(2)]


def step_kernel(got_x, got_z, base, same, factor, stiff, entry, send_x, send_z, edges):
    matches = got_x.shape[1]
    count = 2 * matches
    for part, value in enumerate(new_entries(got_x, got_z, base, same, factor)):
        entry[part] = value
        send_x[part] = value[:matches] * stiff[:matches, :]
        send_z[part] = value[matches:count] * stiff[matches:, :]
    edges[...] = entry[:, count:, :]


def last_kernel(rows, stale, got_x, got_z, base, same, factor, nearby, out, entry, sem):
    for part, value in enumerate(new_entries(got_x, got_z, base, same, factor)):
        entry[part] = value
    stores = load_parts(nearby, out, sem, LOADS)
    for part in range(2):

        def put(slot, row):
            nearby[part, pl.ds(row, 1), :] = entry[part, pl.ds(slot, 1), :]

        each_slot(rows.shape[1], lambda j: rows[0, j], put)
        for copy in stores[part * LOADS : (part + 1) * LOADS]:
            copy.start()
    for copy in stores:
        copy.wait()


def exchange(array, axis, pairs):
    return lax.ppermute(array, axis, pairs)


def pairs_from(first, size):
    out = []
    for i in range(first, size - 1, 2):
        out += [(i, i + 1), (i + 1, i)]
    return out


def on_device(displacement, spring, stiff_table, match_blocks, match_class):
    fields, _, height, breadth = displacement.shape
    chunks = breadth // LANES
    blocks = height * chunks
    matches = match_blocks.shape[2]
    count = 2 * matches
    total = count + 2 * chunks
    sections, tiles = lax.axis_size("sec"), lax.axis_size("tile")
    near, far = pairs_from(0, sections), pairs_from(1, sections)
    near_tile = pairs_from(0, tiles)
    relay = [(i - 1, i + 1) for i in range(1, tiles - 1, 2)] + [(i + 2, i) for i in range(1, tiles - 1, 2)]
    senders, takers = {a for a, _ in relay}, {b for _, b in relay}
    relay += [(b, a) for a, b in relay if b not in senders and a not in takers]

    def tiled(x):
        lead = x.shape[:-2]
        x = x.reshape(lead + (height // SUB, SUB, chunks, LANES))
        return jnp.swapaxes(x, -3, -2).reshape(lead + (blocks, LANES))

    def untiled(x):
        lead = x.shape[:-2]
        x = x.reshape(lead + (height // SUB, chunks, SUB, LANES))
        return jnp.swapaxes(x, -3, -2).reshape(lead + (height, breadth))

    def call(kernel, ins, outs, vmem=24 << 20, **more):
        return pl.pallas_call(
            kernel,
            in_specs=ins,
            out_specs=tuple(spec for spec, _ in outs),
            out_shape=tuple(shape for _, shape in outs),
            compiler_params=pltpu.CompilerParams(vmem_limit_bytes=vmem),
            **more,
        )

    halo = (VM, f32(fields, 2 * chunks, LANES))
    send = (VM, f32(fields, matches, LANES))
    entries = (VM, f32(fields, total, LANES))
    big = (VM, f32(fields, blocks, LANES))
    wide = (VM, f32(total, LANES))
    rows_shape = (VM, jax.ShapeDtypeStruct((1, count), jnp.int32))

    packed = jnp.concatenate([match_blocks, match_class[:, None]], axis=0)
    prev = exchange(packed, "sec", [(i, i + 1) for i in range(sections - 1)])
    staging = [
        pltpu.VMEM((1, matches), jnp.int32),
        pltpu.SMEM((1, matches), jnp.int32),
    ]
    field, own_entry = call(
        functools.partial(own_kernel, chunks),
        [VM, HBM],
        [big, send],
        scratch_shapes=staging + [pltpu.SemaphoreType.DMA, pltpu.SemaphoreType.DMA((2 * LOADS,))],
        vmem=OWN_VMEM << 20,
    )(packed, tiled(displacement[:, 0]))
    entry, stiff, rows, send_x, send_z, edges = call(
        functools.partial(first_kernel, chunks),
        [VM] * 5,
        [entries, (VM, f32(count, LANES)), rows_shape, send, send, halo],
        scratch_shapes=staging
        + [pltpu.VMEM((fields, matches, LANES), jnp.float32), pltpu.SemaphoreType.DMA],
    )(stiff_table[None], packed, prev, field, own_entry)

    for sweep in range(ITERS):
        got_x = exchange(send_x, "sec", near)
        got_z = exchange(send_z, "sec", far)
        got_a = exchange(edges, "tile", near_tile)
        got_b = exchange(got_a, "tile", relay)
        if sweep == 0:
            nearby, base, same, weight, factor = call(
                functools.partial(start_kernel, chunks),
                [SM, VM, VM, VM, VM],
                [big, entries, (VM, jax.ShapeDtypeStruct((total, count + LANES), jnp.bfloat16)), wide, wide],
                scratch_shapes=[pltpu.VMEM((total, LANES), jnp.float32)] * 2,
            )(rows, rows, stiff, tiled(spring[0]), field)
        else:
            field, nearby, base = call(
                functools.partial(scatter_inner_kernel, chunks),
                [SM] + [VM] * 2,
                [big, big, entries],
                input_output_aliases={2: 0},
            )(rows, entry, nearby)
        nearby, base = call(
            functools.partial(settle_kernel, chunks), [VM] * 9, [big, entries], input_output_aliases={8: 0}
        )(got_a, got_b, entry, base, same, weight, factor, stiff, nearby)
        if sweep < ITERS - 1:
            entry, send_x, send_z, edges = call(
                step_kernel, [VM] * 6, [entries, send, send, halo]
            )(got_x, got_z, base, same, factor, stiff)
    _, out = call(
        last_kernel,
        [SM] + [VM] * 6,
        [big, (HBM, f32(fields, blocks, LANES))],
        scratch_shapes=[
            pltpu.VMEM((fields, total, LANES), jnp.float32),
            pltpu.SemaphoreType.DMA((2 * LOADS,)),
        ],
        input_output_aliases={1: 0},
    )(rows, nearby, got_x, got_z, base, same, factor)
    return untiled(out)[:, None]


def solution(mesh):
    placed = (
        P(None, "sec", "tile", None),
        P("sec", "tile", None),
        P(),
        P(None, "sec", "tile"),
        P("sec", "tile"),
    )
    return jax.shard_map(
        on_device,
        mesh=mesh,
        in_specs=placed,
        out_specs=P(None, "sec", "tile", None),
        check_vma=False,
    )
```
